128 devices in a mesh: rows: 128 (over x, y, z, core).
Axes of the slice: x: 4, y: 4, z: 4, core: 2. Of those that a mesh axis runs over, the one named last changes fastest.
Arguments:
- stiffness: float32 [9, 512, 512], P(None, 'rows'), may hold values from -400 to 806.1, as said below
- mass: float32 [9, 512, 512], P(None, 'rows'), may hold values from 0.05 to 3, as said below
- shifts: float32 [3], replicated, may hold values from 0.05 to 2
- factor: float32 [512, 32, 512], P('rows'), may hold values from -6 to 6
Outputs:
- lowrank: float32 [3, 512, 32, 512], P(None, 'rows')
- residual_factor: float32 [512, 32, 512], P('rows')
The draws below stay inside these ranges and needn't reach their ends.
Inputs may be any that keep to these rules, and one draw needn't show every extreme that they name: `stiffness`: entry 4 along the first dimension exceeds the sum of the magnitudes of the other eight, which are negative. `mass`: entry 4 along the first dimension exceeds the sum of the other eight, which are positive.
All inputs are finite; a program needn't handle non-finite values.
Results may differ from the reference program's by a relative error of at most 0.0003.
Values sent between devices are 32-bit elements; how exact they have to be, the bound alone decides.
A program may use at most 128 MiB of HBM per device.

```python
import math
import jax
import jax.numpy as jnp
from jax import lax

NC = 512
NRHS = 32
STEPS = 3
ITERS = 4
NR = 512


def draw_stiffness(key, part):
    key = jax.random.fold_in(key, 11)
    first, second, third = jax.random.split(key, 3)
    others = -(0.2 + 0.8 * jax.random.uniform(first, (6, NR, NC), jnp.float32))
    along = -(100.0 + 300.0 * jax.random.uniform(third, (2, NR, NC), jnp.float32))
    extra = 0.02 + 0.08 * jax.random.uniform(second, (1, NR, NC), jnp.float32)
    center = -jnp.sum(others, axis=0, keepdims=True) - jnp.sum(along, axis=0, keepdims=True) + extra
    return jnp.concatenate([others[:3], along[:1], center, along[1:], others[3:]], axis=0)


def draw_mass(key, part):
    key = jax.random.fold_in(key, 23)
    first, second = jax.random.split(key)
    offdiag = 0.05 + 0.2 * jax.random.uniform(first, (8, NR, NC), jnp.float32)
    extra = 0.2 + 0.8 * jax.random.uniform(second, (1, NR, NC), jnp.float32)
    center = jnp.sum(offdiag, axis=0, keepdims=True) + extra
    return jnp.concatenate([offdiag[:4], center, offdiag[4:]], axis=0)


def level_of(own_key, dims, cuts, smallest, top_value):
    level = 1.0
    for axis_at, parts in cuts:
        draws = jax.random.uniform(jax.random.fold_in(jax.random.fold_in(own_key, 6), axis_at), (parts,), jnp.float32, smallest / len(cuts), top_value / len(cuts))
        level = level * jnp.repeat(jnp.exp(draws), dims[axis_at] // parts).reshape((-1,) + (1,) * (len(dims) - 1 - axis_at))
    return level


def noise(own_key, shape, width, bound, cuts=(), kind=jnp.bfloat16):
    array = width * jax.random.normal(own_key, shape, jnp.float32)
    if cuts:
        array = array * level_of(own_key, shape, cuts, -0.22, 0.18)
    return jnp.clip(array, -bound, bound).astype(kind)


def setup_inputs(seed: int = 0) -> dict:
    splits = jax.random.split(jax.random.key(seed), 5)
    return {
        "stiffness": draw_stiffness(jax.random.fold_in(splits[4], 71), 0),
        "mass": draw_mass(jax.random.fold_in(splits[4], 71), 0),
        "shifts": jnp.clip(jnp.exp(jax.random.uniform(splits[2], (STEPS,), jnp.float32, math.log(0.05), math.log(2.0))), 0.05, 2.0),
        "factor": noise(splits[3], (NR, NRHS, NC), 1.0, 6.0, ((0, 128),), jnp.float32),
    }


OFFSETS = ((-1, -1), (-1, 0), (-1, 1), (0, -1), (0, 0), (0, 1), (1, -1), (1, 0), (1, 1))

def apply_stencil(coeffs, padded):
    height = coeffs.shape[1]
    breadth = padded.shape[2]
    framed = jnp.pad(padded, ((0, 0), (0, 0), (1, 1)))
    summed = jnp.zeros((height, padded.shape[1], breadth), padded.dtype)
    for stencil_entry, offset in enumerate(OFFSETS):
        shifted = framed[1 + offset[0]:1 + offset[0] + height, :, 1 + offset[1]:1 + offset[1] + breadth]
        summed = summed + coeffs[stencil_entry][:, None, :] * shifted
    return summed

def line_solve(coeffs, vector):
    breadth = vector.shape[2]
    column = lax.broadcasted_iota(jnp.int32, (1, breadth), 1)
    below_diag = jnp.where(column == 0, 0.0, coeffs[3]).astype(vector.dtype)
    above_diag = jnp.where(column == breadth - 1, 0.0, coeffs[5]).astype(vector.dtype)
    extent = vector.shape
    below_diag = jnp.broadcast_to(below_diag[:, None, :], extent)
    center = jnp.broadcast_to(coeffs[4][:, None, :], extent)
    above_diag = jnp.broadcast_to(above_diag[:, None, :], extent)
    solved = lax.linalg.tridiagonal_solve(below_diag, center, above_diag, vector[..., None])
    return solved[..., 0]

def pad_rows(field):
    return jnp.pad(field, ((1, 1), (0, 0), (0, 0)))

def row_sums(field):
    return lax.optimization_barrier(jnp.sum(field, axis=(0, 2)))

def least_squares(columns, initial):
    count = len(columns)
    cosines = []
    sines = []
    rhs_list = [initial] + [jnp.zeros_like(initial) for onward in range(count)]
    upper_cols = []
    for position in range(count):
        column = list(columns[position])
        for earlier in range(position):
            first = cosines[earlier] * column[earlier] + sines[earlier] * column[earlier + 1]
            second = -sines[earlier] * column[earlier] + cosines[earlier] * column[earlier + 1]
            column[earlier] = first
            column[earlier + 1] = second
        radius = jnp.sqrt(column[position] * column[position] + column[position + 1] * column[position + 1])
        cosine = column[position] / radius
        sine = column[position + 1] / radius
        cosines.append(cosine)
        sines.append(sine)
        column[position] = radius
        rhs_list[position + 1] = -sine * rhs_list[position]
        rhs_list[position] = cosine * rhs_list[position]
        upper_cols.append(column[:position + 1])
    solution = [None] * count
    for position in reversed(range(count)):
        accum = rhs_list[position]
        for onward in range(position + 1, count):
            accum = accum - upper_cols[onward][position] * solution[onward]
        solution[position] = accum / upper_cols[position][position]
    return solution

def shifted_solve(coeffs, right_side):
    initial = jnp.sqrt(row_sums(right_side * right_side))
    krylov = [right_side / initial[None, :, None]]
    directions = []
    columns = []
    for krylov_step in range(ITERS):
        direction = line_solve(coeffs, krylov[krylov_step])
        directions.append(direction)
        mapped = apply_stencil(coeffs, pad_rows(direction))
        heights = jnp.stack([row_sums(vector * mapped) for vector in krylov])
        for earlier in range(krylov_step + 1):
            mapped = mapped - heights[earlier][None, :, None] * krylov[earlier]
        remainder = jnp.sqrt(row_sums(mapped * mapped))
        columns.append([heights[earlier] for earlier in range(krylov_step + 1)] + [remainder])
        if krylov_step + 1 < ITERS:
            krylov.append(mapped / remainder[None, :, None])
    weights = least_squares(columns, initial)
    result = weights[0][None, :, None] * directions[0]
    for onward in range(1, ITERS):
        result = result + weights[onward][None, :, None] * directions[onward]
    return result

def reference(stiffness, mass, shifts, factor):
    current = factor
    pieces = []
    for adi_step in range(STEPS):
        shift_now = shifts[adi_step]
        coeffs = stiffness + shift_now * mass
        result = shifted_solve(coeffs, current)
        pieces.append(jnp.sqrt(2.0 * shift_now) * result)
        current = current - 2.0 * shift_now * apply_stencil(mass, pad_rows(result))
    return (jnp.stack(pieces), current)
```

```python
import functools

import jax
import jax.numpy as jnp
from jax import lax
from jax.experimental import pallas as pl
from jax.experimental.pallas import tpu as pltpu
from jax.sharding import PartitionSpec as P

STEPS = 3
ITERS = 4
MESH = pl.DeviceIdType.MESH
PAIRS = [(i, j) for i in range(ITERS + 1) for j in range(i, ITERS + 1)]
LANES = 128
CHUNK = 4
F32 = jnp.float32
BF16 = jnp.bfloat16

NAMES = ["w1", "w2", "i0", "i1", "i2", "c0", "c1", "a3", "c3", "e0", "e1", "e2", "f0", "f1", "f2", "inv"]
NAMES += ["al%d" % n for n in range(7)] + ["ga%d" % n for n in range(7)]
SLOT = {name: n for n, name in enumerate(NAMES)}
OFF = (0, 1, 2, 6, 7, 8)


def lane_roll(x, shift):
    return pltpu.roll(x, shift % LANES, axis=x.ndim - 1)


def split3(x):
    a = x.astype(BF16)
    rest = x - a.astype(F32)
    b = rest.astype(BF16)
    c = (rest - b.astype(F32)).astype(BF16)
    return a, b, c


def permuted(x, perm, dim):
    total = None
    for part in split3(x):
        term = lax.dot_general(part, perm, (((1,), (dim,)), ((), ())), preferred_element_type=F32)
        total = term if total is None else total + term
    return total


def line_factors(a, b, c):
    out = {}
    i0 = 1.0 / b[0]
    w1 = a[1] * i0
    i1 = 1.0 / (b[1] - w1 * c[0])
    w2 = a[2] * i1
    i2 = 1.0 / (b[2] - w2 * c[1])
    t1 = -w1 * a[0]
    e2 = -w2 * t1 * i2
    e1 = (t1 - c[1] * e2) * i1
    e0 = (a[0] - c[0] * e1) * i0
    f2 = c[2] * i2
    f1 = -c[1] * f2 * i1
    f0 = -c[0] * f1 * i0
    out.update(w1=w1, w2=w2, i0=i0, i1=i1, i2=i2, c0=c[0], c1=c[1], a3=a[3], c3=c[3])
    out.update(e0=e0, e1=e1, e2=e2, f0=f0, f1=f1, f2=f2)
    low = -a[3] * e2
    mid = b[3] - a[3] * f2 - c[3] * lane_roll(e0, -1)
    high = -c[3] * lane_roll(f0, -1)
    for level in range(7):
        k = 1 << level
        inv = 1.0 / mid
        al = -low * lane_roll(inv, k)
        ga = -high * lane_roll(inv, -k)
        mid = mid + al * lane_roll(high, k) + ga * lane_roll(low, -k)
        low, high = al * lane_roll(low, k), ga * lane_roll(high, -k)
        out["al%d" % level] = al
        out["ga%d" % level] = ga
    out["inv"] = 1.0 / mid
    return out


def least_squares(columns, initial):
    count = len(columns)
    cosines, sines = [], []
    rhs = [initial] + [None] * count
    upper = []
    for position in range(count):
        column = list(columns[position])
        for earlier in range(position):
            first = cosines[earlier] * column[earlier] + sines[earlier] * column[earlier + 1]
            second = -sines[earlier] * column[earlier] + cosines[earlier] * column[earlier + 1]
            column[earlier], column[earlier + 1] = first, second
        radius = jnp.sqrt(column[position] * column[position] + column[position + 1] * column[position + 1])
        inverse = 1.0 / radius
        cosine = column[position] * inverse
        sine = column[position + 1] * inverse
        cosines.append(cosine)
        sines.append(sine)
        rhs[position + 1] = -sine * rhs[position]
        rhs[position] = cosine * rhs[position]
        upper.append(column[:position] + [inverse])
    y = [None] * count
    for position in reversed(range(count)):
        accum = rhs[position]
        for onward in range(position + 1, count):
            accum = accum - upper[onward][position] * y[onward]
        y[position] = accum * upper[position][position]
    return y


def solve_weights(gram):
    n = ITERS + 1
    r = {}
    for i in range(n):
        pivot = gram[(i, i)]
        for m in range(i):
            pivot = pivot - r[(m, i)] * r[(m, i)]
        pivot = jnp.maximum(pivot, gram[(i, i)] * 1e-9)
        root = jnp.sqrt(pivot)
        r[(i, i)] = root
        inverse = 1.0 / root
        for j in range(i + 1, n):
            value = gram[(i, j)]
            for m in range(i):
                value = value - r[(m, i)] * r[(m, j)]
            r[(i, j)] = value * inverse
    columns = []
    for k in range(ITERS):
        columns.append([r[(i, k)] + r[(i, k + 1)] for i in range(k + 1)] + [r[(k + 1, k + 1)]])
    return least_squares(columns, r[(0, 0)])


def kernel(chips, shifts, stiff_hbm, mass_hbm, factor_hbm, low_hbm, res_hbm,
           perm, raw_s, raw_m, raw_w, lhs, ce, fc, pb, zb, ub, us, os_, arb, hx, msg,
           in_send, in_recv, far_send, ar_send, ar_recv, hx_send, hx_recv, out_send, out_recv, out_local):
    me = lax.axis_index("rows")
    k = me // 2
    c = me % 2
    up = lax.rem(k + chips - 1, chips)
    down = lax.rem(k + 1, chips)

    def device(chip, core):
        return (chip * 2 + core,)

    barrier = pltpu.get_barrier_semaphore()

    def greet(n, carry):
        pl.semaphore_signal(barrier, inc=1, device_id=device(lax.rem(k + n, chips), c), device_id_type=MESH)
        return carry

    for chip in (k, up, down):
        pl.semaphore_signal(barrier, inc=1, device_id=device(chip, 1 - c), device_id_type=MESH)
    lax.fori_loop(1, chips, greet, 0)

    own = 2 + c
    own_copies = [
        pltpu.make_async_copy(stiff_hbm, raw_s.at[own], in_recv.at[own, 0]),
        pltpu.make_async_copy(mass_hbm, raw_m.at[own], in_recv.at[own, 1]),
        pltpu.make_async_copy(factor_hbm.at[:, pl.ds(pl.multiple_of(16 * c, 16), 16), :], raw_w.at[own], in_recv.at[own, 2]),
    ]
    for copy in own_copies:
        copy.start()

    row = lax.broadcasted_iota(jnp.int32, (512, 512), 0)
    col = lax.broadcasted_iota(jnp.int32, (512, 512), 1)
    perm[...] = jnp.where(row == CHUNK * (col % LANES) + col // LANES, 1.0, 0.0).astype(BF16)

    pl.semaphore_wait(barrier, chips - 1 + 3)

    def block_copies(chip, core, block, sems):
        return [
            pltpu.make_async_remote_copy(
                src_ref=factor_hbm.at[:, pl.ds(pl.multiple_of(16 * core, 16), 16), :], dst_ref=raw_w.at[block],
                send_sem=sems.at[2], recv_sem=in_recv.at[block, 2], device_id=device(chip, core), device_id_type=MESH),
            pltpu.make_async_remote_copy(
                src_ref=stiff_hbm, dst_ref=raw_s.at[block],
                send_sem=sems.at[0], recv_sem=in_recv.at[block, 0], device_id=device(chip, core), device_id_type=MESH),
            pltpu.make_async_remote_copy(
                src_ref=mass_hbm, dst_ref=raw_m.at[block],
                send_sem=sems.at[1], recv_sem=in_recv.at[block, 1], device_id=device(chip, core), device_id_type=MESH),
        ]

    near_chip = lax.rem(k + 2 * c - 1 + chips, chips)
    far_chip = lax.rem(k + 1 - 2 * c + chips, chips)
    near_copies = []
    for core in range(2):
        near_copies += block_copies(near_chip, core, 4 - 3 * c, in_send.at[core])
    near_copies += block_copies(k, 1 - c, own, in_send.at[2])
    far_copies = []
    for core in range(2):
        far_copies += block_copies(far_chip, core, 5 * c, far_send.at[core])
    for copy in near_copies:
        copy.start()

    def wait_block(block):
        pltpu.make_async_copy(raw_s.at[block], raw_s.at[block], in_recv.at[block, 0]).wait()
        pltpu.make_async_copy(raw_m.at[block], raw_m.at[block], in_recv.at[block, 1]).wait()
        pltpu.make_async_copy(raw_w.at[block], raw_w.at[block], in_recv.at[block, 2]).wait()

    first = k == 0
    last = k == chips - 1
    lane = lax.broadcasted_iota(jnp.int32, (1, LANES), 1)

    def absent(block):
        if block < 2:
            return first
        if block > 3:
            return last
        return None

    def prepare(blocks, base, rows):
        count = 4 * len(blocks)
        for e in range(18):
            for n, block in enumerate(blocks):
                value = (raw_s if e < 9 else raw_m)[block, e % 9]
                gone = absent(block)
                if gone is not None:
                    value = jnp.where(gone, 1.0 if e == 4 else 0.0, value)
                lhs[e * count + 4 * n:e * count + 4 * n + 4, :] = value
        moved = permuted(lhs[0:18 * count, :], perm[...], 0)
        for e in range(18):
            for m in range(CHUNK):
                value = moved[e * count:(e + 1) * count, m * LANES:(m + 1) * LANES]
                if m == 0 and e % 3 == 0:
                    value = jnp.where(lane == 0, 0.0, value)
                if m == CHUNK - 1 and e % 3 == 2:
                    value = jnp.where(lane == LANES - 1, 0.0, value)
                ce[e * CHUNK + m, base:base + count, :] = value
        for n, block in enumerate(blocks):
            value = raw_w[block].reshape(64, 512)
            gone = absent(block)
            if gone is not None:
                value = jnp.where(gone, 0.0, value)
            value = permuted(value, perm[...], 0)
            for r in range(4):
                for half in range(2):
                    for m in range(CHUNK):
                        pb[0, rows[n] + r, m, half] = value[16 * r + 8 * half:16 * r + 8 * half + 8, m * LANES:(m + 1) * LANES]

    def factor_rows(s, lo, hi):
        def entry(e, m):
            return ce[e * CHUNK + m, lo:hi, :] + s * ce[(9 + e) * CHUNK + m, lo:hi, :]
        parts = line_factors(*[[entry(e, m) for m in range(CHUNK)] for e in (3, 4, 5)])
        for name, value in parts.items():
            fc[SLOT[name], lo:hi, :] = value
        for n, e in enumerate(OFF):
            for m in range(CHUNK):
                fc[len(NAMES) + n * CHUNK + m, lo:hi, :] = entry(e, m)

    def slot_of(r):
        return jnp.where(r < 4, r + 16, jnp.where(r < 20, r - 4, r))

    def spread(ref, index, slot):
        return ref[index, pl.ds(slot, 1), :][None]

    def line_group(it, r0, count=4):
        rows = [r0 + n for n in range(count)]
        slots = [slot_of(r) for r in rows]

        def co(name, n):
            return spread(fc, SLOT[name], slots[n])

        g, d = [], []
        for n, r in enumerate(rows):
            d0, d1, d2, d3 = [pb[it, r, m] for m in range(CHUNK)]
            d1 = d1 - co("w1", n) * d0
            d2 = d2 - co("w2", n) * d1
            g2 = d2 * co("i2", n)
            g1 = (d1 - co("c1", n) * g2) * co("i1", n)
            g0 = (d0 - co("c0", n) * g1) * co("i0", n)
            d.append(d3 - co("a3", n) * g2 - co("c3", n) * lane_roll(g0, -1))
            g.append((g0, g1, g2))
        for level in range(7):
            step = 1 << level
            d = [v + co("al%d" % level, n) * lane_roll(v, step) + co("ga%d" % level, n) * lane_roll(v, -step)
                 for n, v in enumerate(d)]
        for n, r in enumerate(rows):
            x3 = d[n] * co("inv", n)
            before = lane_roll(x3, 1)
            x0 = g[n][0] - co("e0", n) * before - co("f0", n) * x3
            x1 = g[n][1] - co("e1", n) * before - co("f1", n) * x3
            x2 = g[n][2] - co("e2", n) * before - co("f2", n) * x3
            zb[it, r, 0] = before
            zb[it, r, 1] = x0
            zb[it, r, 2] = x1
            zb[it, r, 3] = x2
            zb[it, r, 4] = x3
            zb[it, r, 5] = lane_roll(x0, -1)

    def off_row(it, r):
        slot = slot_of(r)
        for m in range(CHUNK):
            total = None
            for n, e in enumerate(OFF):
                source = zb[it, r + (-1 if e < 3 else 1), m + e % 3]
                term = spread(fc, len(NAMES) + n * CHUNK + m, slot) * source
                total = term if total is None else total + term
            pb[it + 1, r, m] = total

    def send_halo(do):
        for n, (chip, at) in enumerate(((down, 8), (up, 12))):
            copy = pltpu.make_async_remote_copy(
                src_ref=pb.at[0, pl.ds(at, 4)], dst_ref=hx.at[n], send_sem=hx_send.at[n], recv_sem=hx_recv.at[n],
                device_id=device(chip, c), device_id_type=MESH)
            do(copy)

    def ar_copy(t, n):
        return pltpu.make_async_remote_copy(
            src_ref=msg.at[t], dst_ref=arb.at[t, k], send_sem=ar_send.at[t], recv_sem=ar_recv.at[t],
            device_id=device(lax.rem(k + n, chips), c), device_id_type=MESH)

    def out_copies(n, dst_local, dst_remote):
        return (
            pltpu.make_async_copy(os_.at[n, pl.ds(4 * c, 4)], dst_local, out_local.at[n]),
            pltpu.make_async_remote_copy(
                src_ref=os_.at[n, pl.ds(4 - 4 * c, 4)], dst_ref=dst_remote, send_sem=out_send.at[n], recv_sem=out_recv.at[n],
                device_id=device(k, 1 - c), device_id_type=MESH),
        )

    half_cols = pl.ds(pl.multiple_of(16 * c, 16), 16)

    def out_ref(n):
        return low_hbm.at[n, :, half_cols, :]

    def native(source):
        flat = jnp.concatenate([source[:, m].reshape(128, LANES) for m in range(CHUNK)], axis=1)
        return permuted(flat, perm[...], 1).reshape(8, 16, 512)

    def emit_low(n):
        os_[n] = native(us[...])
        for copy in out_copies(n, out_ref(n), out_ref(n)):
            copy.start()

    for block in (2, 3, 1, 4):
        wait_block(block)
    for copy in far_copies:
        copy.start()
    prepare((1, 2, 3, 4), 0, (4, 8, 12, 16))

    lane8 = lax.broadcasted_iota(jnp.int32, (8, LANES), 1)

    def adi(t, carry):
        s = shifts[t]

        @pl.when(t == 1)
        def _():
            send_halo(lambda copy: copy.start())

        factor_rows(s, 0, 16)

        def main(it, carry):
            def groups(n, carry):
                line_group(it, jnp.minimum(4 + it + 4 * n, 16 - it))
                return carry
            lax.fori_loop(0, 4 - it // 2, groups, 0)

            def rows(n, carry):
                off_row(it, 5 + it + 2 * n)
                off_row(it, 6 + it + 2 * n)
                return carry
            lax.fori_loop(0, 7 - it, rows, 0)
            return carry
        lax.fori_loop(0, ITERS, main, 0)

        def dots(r, sums):
            sums = list(sums)
            for m in range(CHUNK):
                v = [pb[i, r, m] for i in range(ITERS + 1)]
                sums = [old + v[i] * v[j] for old, (i, j) in zip(sums, PAIRS)]
            return tuple(sums)
        sums = lax.fori_loop(8, 16, dots, tuple(jnp.zeros((2, 8, LANES), F32) for _ in PAIRS))
        packed = jnp.zeros((8, LANES), F32)
        for n, value in enumerate(sums):
            value = jnp.sum(value, axis=2, keepdims=True)
            for half in range(2):
                packed = jnp.where(lane8 == 16 * half + n, value[half], packed)
        msg[t] = packed
        arb[t, k] = packed

        def send(n, carry):
            ar_copy(t, n).start()
            return carry
        lax.fori_loop(1, chips, send, 0)

        @pl.when(t == 0)
        def _():
            wait_block(0)
            wait_block(5)
            prepare((0, 5), 16, (0, 20))

        @pl.when(t > 0)
        def _():
            emit_low(t - 1)

        @pl.when(t == 1)
        def _():
            send_halo(lambda copy: copy.wait())
            for n, at in enumerate((0, 20)):
                gone = first if n == 0 else last
                for r in range(4):
                    pb[0, at + r] = jnp.where(gone, 0.0, hx[n, r])

        @pl.when(t < 2)
        def _():
            factor_rows(s, 16, 24)

            def outer(it, carry):
                def side(n, carry):
                    line_group(it, jnp.where(n == 0, it, 20 - it))
                    return carry
                lax.fori_loop(0, 2, side, 0)

                @pl.when(it < ITERS - 1)
                def _():
                    def rows(n, carry):
                        off_row(it, it + 1 + n)
                        off_row(it, 19 - it + n)
                        return carry
                    lax.fori_loop(0, 4, rows, 0)
                return carry
            lax.fori_loop(0, ITERS, outer, 0)

        pltpu.make_async_copy(arb.at[t, pl.ds(0, chips - 1)], arb.at[t, pl.ds(0, chips - 1)], ar_recv.at[t]).wait()
        total = jnp.sum(arb[t], axis=0)
        gram = {}
        for n, pair in enumerate(PAIRS):
            gram[pair] = jnp.stack([
                jnp.broadcast_to(jnp.sum(jnp.where(lane8 == 16 * half + n, total, 0.0), axis=1, keepdims=True), (8, LANES))
                for half in range(2)])
        y = solve_weights(gram)
        scale = jnp.sqrt(jnp.full((1, 8, LANES), 2.0 * s, F32))

        def combine(r, carry):
            for m in range(6):
                total = y[0] * zb[0, r, m]
                for it in range(1, ITERS):
                    total = total + y[it] * zb[it, r, m]
                ub[r, m] = total
            return carry
        lax.fori_loop(jnp.where(t < 2, 3, 7), jnp.where(t < 2, 21, 17), combine, 0)

        def keep(r, carry):
            for m in range(CHUNK):
                us[r, m] = scale * ub[8 + r, 1 + m]
            return carry
        lax.fori_loop(0, 8, keep, 0)

        twice = 2.0 * s

        def update(r, carry):
            slot = slot_of(r)
            for m in range(CHUNK):
                total = None
                for e in range(9):
                    term = spread(ce, (9 + e) * CHUNK + m, slot) * ub[r + e // 3 - 1, m + e % 3]
                    total = term if total is None else total + term
                pb[0, r, m] = pb[0, r, m] - twice * total
            return carry
        lax.fori_loop(jnp.where(t < 2, 4, 8), jnp.where(t < 2, 20, 16), update, 0)
        return carry

    lax.fori_loop(0, STEPS, adi, 0)

    emit_low(STEPS - 1)
    os_[STEPS] = native(pb[0, 8:16])
    res_at = res_hbm.at[:, half_cols, :]
    for copy in out_copies(STEPS, res_at, res_at):
        copy.start()

    for copy in near_copies + far_copies:
        copy.wait_send()

    def drain(t, carry):
        pltpu.make_async_copy(arb.at[t, pl.ds(0, chips - 1)], arb.at[t, pl.ds(0, chips - 1)], ar_send.at[t]).wait()
        for copy in out_copies(t, out_ref(t), out_ref(t)):
            copy.wait()
        return carry
    lax.fori_loop(0, STEPS, drain, 0)
    for copy in out_copies(STEPS, res_at, res_at):
        copy.wait()


def solution(mesh):
    chips = mesh.shape["rows"] // 2

    def shards(stiffness, mass, shifts, factor):
        field = (24, CHUNK, 2, 8, LANES)
        framed = (24, CHUNK + 2, 2, 8, LANES)
        dma = pltpu.SemaphoreType.DMA
        return pl.pallas_call(
            functools.partial(kernel, chips),
            out_shape=(jax.ShapeDtypeStruct((STEPS, 4, 32, 512), F32), jax.ShapeDtypeStruct((4, 32, 512), F32)),
            in_specs=[pl.BlockSpec(memory_space=pltpu.SMEM)] + [pl.BlockSpec(memory_space=pl.ANY)] * 3,
            out_specs=(pl.BlockSpec(memory_space=pl.ANY), pl.BlockSpec(memory_space=pl.ANY)),
            scratch_shapes=[
                pltpu.VMEM((512, 512), BF16),
                pltpu.VMEM((6, 9, 4, 512), F32),
                pltpu.VMEM((6, 9, 4, 512), F32),
                pltpu.VMEM((6, 4, 16, 512), F32),
                pltpu.VMEM((18 * 16, 512), F32),
                pltpu.VMEM((18 * CHUNK, 24, LANES), F32),
                pltpu.VMEM((len(NAMES) + 6 * CHUNK, 24, LANES), F32),
                pltpu.VMEM((ITERS + 1,) + field, F32),
                pltpu.VMEM((ITERS,) + framed, F32),
                pltpu.VMEM(framed, F32),
                pltpu.VMEM((8, CHUNK, 2, 8, LANES), F32),
                pltpu.VMEM((STEPS + 1, 8, 16, 512), F32),
                pltpu.VMEM((STEPS, chips, 8, LANES), F32),
                pltpu.VMEM((2, 4, CHUNK, 2, 8, LANES), F32),
                pltpu.VMEM((STEPS, 8, LANES), F32),
                dma((3, 3)),
                dma((6, 3)),
                dma((2, 3)),
                dma((STEPS,)),
                dma((STEPS,)),
                dma((2,)),
                dma((2,)),
                dma((STEPS + 1,)),
                dma((STEPS + 1,)),
                dma((STEPS + 1,)),
            ],
            compiler_params=pltpu.CompilerParams(
                collective_id=0, has_side_effects=True, vmem_limit_bytes=48 << 20),
        )(shifts, stiffness, mass, factor)

    return jax.shard_map(
        shards,
        mesh=mesh,
        in_specs=(P(None, "rows", None), P(None, "rows", None), P(), P("rows", None, None)),
        out_specs=(P(None, "rows", None, None), P("rows", None, None)),
        check_vma=False,
    )
```

```python
import functools

import jax
import jax.numpy as jnp
from jax import lax
from jax.experimental import pallas as pl
from jax.experimental.pallas import tpu as pltpu
from jax.sharding import PartitionSpec as P

STEPS = 3
ITERS = 4
MESH = pl.DeviceIdType.MESH
PAIRS = [(i, j) for i in range(ITERS + 1) for j in range(i, ITERS + 1)]
LANES = 128
CHUNK = 8
HALF = 64
F32 = jnp.float32
BF16 = jnp.bfloat16

NAMES = ["w%d" % n for n in range(1, 7)] + ["i%d" % n for n in range(7)] + ["u%d" % n for n in range(6)]
NAMES += ["e%d" % n for n in range(7)] + ["f%d" % n for n in range(7)] + ["a7", "c7", "inv"]
NAMES += ["p%d%s%d" % (level, way, reach) for level in range(3) for way in "du" for reach in (1, 2, 3)]
SLOT = {name: n for n, name in enumerate(NAMES)}
OFF = (0, 1, 2, 6, 7, 8)
COUNT = len(NAMES) + len(OFF) * CHUNK


def lane_roll(x, shift):
    return pltpu.roll(x, shift % LANES, axis=x.ndim - 1)


def split3(x):
    a = x.astype(BF16)
    rest = x - a.astype(F32)
    b = rest.astype(BF16)
    c = (rest - b.astype(F32)).astype(BF16)
    return a, b, c


def permuted(x, perm, dim=0):
    total = None
    for part in split3(x):
        term = lax.dot_general(part, perm, (((1,), (dim,)), ((), ())), preferred_element_type=F32)
        total = term if total is None else total + term
    return total


def line_factors(a, b, c):
    out = {}
    last = CHUNK - 1
    i, u, w = [], [], [None]
    for m in range(last):
        pivot = b[m]
        if m:
            w.append(a[m] * i[m - 1])
            pivot = pivot - w[m] * c[m - 1]
        i.append(1.0 / pivot)
        u.append(c[m] * i[m])
    t = [a[0]]
    for m in range(1, last):
        t.append(-w[m] * t[m - 1])
    e, f = [None] * last, [None] * last
    e[last - 1] = t[last - 1] * i[last - 1]
    f[last - 1] = u[last - 1]
    for m in reversed(range(last - 1)):
        e[m] = t[m] * i[m] - u[m] * e[m + 1]
        f[m] = -u[m] * f[m + 1]
    for m in range(last):
        out["i%d" % m], out["e%d" % m], out["f%d" % m] = i[m], e[m], f[m]
        if m:
            out["w%d" % m] = w[m]
        if m < last - 1:
            out["u%d" % m] = u[m]
    out["a7"], out["c7"] = a[last], c[last]
    low = -a[last] * e[last - 1]
    mid = b[last] - a[last] * f[last - 1] - c[last] * lane_roll(e[0], -1)
    high = -c[last] * lane_roll(f[0], -1)
    for level in range(3):
        k = 1 << (2 * level)
        pairs = []
        for reach in (k, 2 * k):
            inv = 1.0 / mid
            al = -low * lane_roll(inv, reach)
            ga = -high * lane_roll(inv, -reach)
            mid = mid + al * lane_roll(high, reach) + ga * lane_roll(low, -reach)
            low, high = al * lane_roll(low, reach), ga * lane_roll(high, -reach)
            pairs.append((al, ga))
        (al1, ga1), (al2, ga2) = pairs
        merged = {
            "d1": al1 + al2 * lane_roll(ga1, 2 * k), "d2": al2, "d3": al2 * lane_roll(al1, 2 * k),
            "u1": ga1 + ga2 * lane_roll(al1, -2 * k), "u2": ga2, "u3": ga2 * lane_roll(ga1, -2 * k),
        }
        for key, value in merged.items():
            out["p%d%s" % (level, key)] = value
    inv = 1.0 / mid
    out["inv"] = inv
    for key in ("d1", "d2", "d3", "u1", "u2", "u3"):
        out["p2" + key] = out["p2" + key] * inv
    return out


def least_squares(columns, initial):
    count = len(columns)
    cosines, sines = [], []
    rhs = [initial] + [None] * count
    upper = []
    for position in range(count):
        column = list(columns[position])
        for earlier in range(position):
            first = cosines[earlier] * column[earlier] + sines[earlier] * column[earlier + 1]
            second = -sines[earlier] * column[earlier] + cosines[earlier] * column[earlier + 1]
            column[earlier], column[earlier + 1] = first, second
        radius = jnp.sqrt(column[position] * column[position] + column[position + 1] * column[position + 1])
        inverse = 1.0 / radius
        cosine = column[position] * inverse
        sine = column[position + 1] * inverse
        cosines.append(cosine)
        sines.append(sine)
        rhs[position + 1] = -sine * rhs[position]
        rhs[position] = cosine * rhs[position]
        upper.append(column[:position] + [inverse])
    y = [None] * count
    for position in reversed(range(count)):
        accum = rhs[position]
        for onward in range(position + 1, count):
            accum = accum - upper[onward][position] * y[onward]
        y[position] = accum * upper[position][position]
    return y


def solve_weights(gram):
    n = ITERS + 1
    r = {}
    for i in range(n):
        pivot = gram[(i, i)]
        for m in range(i):
            pivot = pivot - r[(m, i)] * r[(m, i)]
        pivot = jnp.maximum(pivot, gram[(i, i)] * 1e-9)
        root = jnp.sqrt(pivot)
        r[(i, i)] = root
        inverse = 1.0 / root
        for j in range(i + 1, n):
            value = gram[(i, j)]
            for m in range(i):
                value = value - r[(m, i)] * r[(m, j)]
            r[(i, j)] = value * inverse
    columns = []
    for k in range(ITERS):
        columns.append([r[(i, k)] + r[(i, k + 1)] for i in range(k + 1)] + [r[(k + 1, k + 1)]])
    return least_squares(columns, r[(0, 0)])


def kernel(chips, shifts, stiff_hbm, mass_hbm, factor_hbm, low_hbm, res_hbm,
           perm, own_s, own_m, own_w, lhs, send_c, send_w, raw_c, ce, fc, pb, zb, ub, us, os_, arb, hx, msg,
           own_sem, in_send, in_recv, far_send, ar_send, ar_recv, hx_send, hx_recv, out_send, out_recv, out_local):
    me = lax.axis_index("rows")
    k = me // 2
    c = me % 2
    up = lax.rem(k + chips - 1, chips)
    down = lax.rem(k + 1, chips)

    def device(chip, core):
        return (chip * 2 + core,)

    barrier = pltpu.get_barrier_semaphore()

    def greet(n, carry):
        pl.semaphore_signal(barrier, inc=1, device_id=device(lax.rem(k + n, chips), c), device_id_type=MESH)
        return carry

    for chip in (k, up, down):
        pl.semaphore_signal(barrier, inc=1, device_id=device(chip, 1 - c), device_id_type=MESH)
    lax.fori_loop(1, chips, greet, 0)

    own_copies = [
        pltpu.make_async_copy(stiff_hbm, own_s, own_sem.at[0]),
        pltpu.make_async_copy(mass_hbm, own_m, own_sem.at[1]),
        pltpu.make_async_copy(factor_hbm, own_w, own_sem.at[2]),
    ]
    for copy in own_copies:
        copy.start()

    row = lax.broadcasted_iota(jnp.int32, (512, CHUNK * LANES), 0)
    col = lax.broadcasted_iota(jnp.int32, (512, CHUNK * LANES), 1)
    perm[...] = jnp.where(row == CHUNK * (col % HALF) + col // LANES, 1.0, 0.0).astype(BF16)

    lane = lax.broadcasted_iota(jnp.int32, (8, LANES), 1)
    left = lane < HALF
    lane1 = lax.broadcasted_iota(jnp.int32, (1, LANES), 1)
    left1 = lane1 < HALF
    first = k == 0
    last = k == chips - 1
    own = 2 + c

    for copy in own_copies:
        copy.wait()
    for e in range(18):
        lhs[4 * e:4 * e + 4, :] = own_s[e] if e < 9 else own_m[e - 9]
    moved = permuted(lhs[0:72, :], perm[...])
    for q in range(4):
        send_c[:, q * LANES:(q + 1) * LANES] = jnp.where(
            left1, moved[:, 2 * q * LANES:(2 * q + 1) * LANES], moved[:, (2 * q + 1) * LANES:(2 * q + 2) * LANES])
    moved = permuted(own_w[...].reshape(128, 512), perm[...])
    for core in range(2):
        for r in range(4):
            at = 32 * r + 16 * core
            for m in range(CHUNK):
                span = slice(m * LANES, (m + 1) * LANES)
                send_w[core, r, m] = jnp.where(left, moved[at:at + 8, span], moved[at + 8:at + 16, span])
    raw_c[own] = send_c[...]
    pb[0, pl.ds(4 * own, 4)] = send_w[c]

    pl.semaphore_wait(barrier, chips - 1 + 3)

    def block_copies(chip, core, block, sems):
        return [
            pltpu.make_async_remote_copy(
                src_ref=send_c, dst_ref=raw_c.at[block],
                send_sem=sems.at[0], recv_sem=in_recv.at[block, 0], device_id=device(chip, core), device_id_type=MESH),
            pltpu.make_async_remote_copy(
                src_ref=send_w.at[core], dst_ref=pb.at[0, pl.ds(4 * block, 4)],
                send_sem=sems.at[1], recv_sem=in_recv.at[block, 1], device_id=device(chip, core), device_id_type=MESH),
        ]

    near_chip = lax.rem(k + 2 * c - 1 + chips, chips)
    far_chip = lax.rem(k + 1 - 2 * c + chips, chips)
    near_copies = []
    for core in range(2):
        near_copies += block_copies(near_chip, core, 4 - 3 * c, in_send.at[core])
    near_copies += block_copies(k, 1 - c, own, in_send.at[2])
    far_copies = []
    for core in range(2):
        far_copies += block_copies(far_chip, core, 5 * c, far_send.at[core])
    for copy in near_copies:
        copy.start()

    def wait_block(block):
        pltpu.make_async_copy(raw_c.at[block], raw_c.at[block], in_recv.at[block, 0]).wait()
        rows = pb.at[0, pl.ds(4 * block, 4)]
        pltpu.make_async_copy(rows, rows, in_recv.at[block, 1]).wait()

    def absent(block):
        if block < 2:
            return first
        if block > 3:
            return last
        return None

    def prepare(blocks, base):
        count = 4 * len(blocks)
        for e in range(18):
            for n, block in enumerate(blocks):
                value = raw_c[block, 4 * e:4 * e + 4, :]
                gone = absent(block)
                if gone is not None:
                    value = jnp.where(gone, 1.0 if e == 4 else 0.0, value)
                lhs[e * count + 4 * n:e * count + 4 * n + 4, :] = value
        for e in range(18):
            for q in range(4):
                value = lhs[e * count:(e + 1) * count, q * LANES:(q + 1) * LANES]
                other = lane_roll(value, HALF)
                both = [jnp.where(left1, value, other), jnp.where(left1, other, value)]
                if q == 0 and e % 3 == 0:
                    both[0] = jnp.where(lane1 % HALF == 0, 0.0, both[0])
                if q == 3 and e % 3 == 2:
                    both[1] = jnp.where(lane1 % HALF == HALF - 1, 0.0, both[1])
                for n in range(2):
                    ce[e * CHUNK + 2 * q + n, base:base + count, :] = both[n]
        for block in blocks:
            gone = absent(block)
            if gone is not None:
                @pl.when(gone)
                def _():
                    pb[0, 4 * block:4 * block + 4] = jnp.zeros((4, CHUNK, 8, LANES), F32)

    def factor_rows(t, lo, hi):
        s = shifts[t]
        par = lax.rem(t, 2)

        def entry(e, m):
            return ce[e * CHUNK + m, lo:hi, :] + s * ce[(9 + e) * CHUNK + m, lo:hi, :]
        parts = line_factors(*[[entry(e, m) for m in range(CHUNK)] for e in (3, 4, 5)])
        for name, value in parts.items():
            fc[par, SLOT[name], lo:hi, :] = value
        for n, e in enumerate(OFF):
            for m in range(CHUNK):
                fc[par, len(NAMES) + n * CHUNK + m, lo:hi, :] = entry(e, m)

    def slot_of(r):
        return jnp.where(r < 4, r + 16, jnp.where(r < 20, r - 4, r))

    def line_group(par, it, rows):
        slots = [slot_of(r) for r in rows]

        def co(name, n):
            return fc[par, SLOT[name], pl.ds(slots[n], 1), :]

        g, d = [], []
        for n, r in enumerate(rows):
            v = [pb[it, r, m] for m in range(CHUNK)]
            for m in range(1, CHUNK - 1):
                v[m] = v[m] - co("w%d" % m, n) * v[m - 1]
            x = [v[m] * co("i%d" % m, n) for m in range(CHUNK - 1)]
            for m in reversed(range(CHUNK - 2)):
                x[m] = x[m] - co("u%d" % m, n) * x[m + 1]
            d.append(v[-1] - co("a7", n) * x[-1] - co("c7", n) * lane_roll(x[0], -1))
            g.append(x)
        for level in range(3):
            step = 1 << (2 * level)
            new = []
            for n, v in enumerate(d):
                total = v if level < 2 else v * co("inv", n)
                for reach in (1, 2, 3):
                    total = total + (co("p%dd%d" % (level, reach), n) * lane_roll(v, reach * step)
                                     + co("p%du%d" % (level, reach), n) * lane_roll(v, -reach * step))
                new.append(total)
            d = new
        for n, r in enumerate(rows):
            after = d[n]
            before = lane_roll(after, 1)
            zb[it, r, 0] = before
            zb[it, r, CHUNK] = after
            for m in range(CHUNK - 1):
                value = g[n][m] - co("e%d" % m, n) * before - co("f%d" % m, n) * after
                zb[it, r, m + 1] = value
                if m == 0:
                    zb[it, r, CHUNK + 1] = lane_roll(value, -1)

    def off_row(par, it, r):
        slot = slot_of(r)
        for m in range(CHUNK):
            total = None
            for n, e in enumerate(OFF):
                source = zb[it, r + (-1 if e < 3 else 1), m + e % 3]
                term = fc[par, len(NAMES) + n * CHUNK + m, pl.ds(slot, 1), :] * source
                total = term if total is None else total + term
            pb[it + 1, r, m] = total

    def send_halo(do):
        for n, (chip, at) in enumerate(((down, 8), (up, 12))):
            copy = pltpu.make_async_remote_copy(
                src_ref=pb.at[0, pl.ds(at, 4)], dst_ref=hx.at[n], send_sem=hx_send.at[n], recv_sem=hx_recv.at[n],
                device_id=device(chip, c), device_id_type=MESH)
            do(copy)

    def ar_copy(t, n):
        return pltpu.make_async_remote_copy(
            src_ref=msg.at[t], dst_ref=arb.at[t, k], send_sem=ar_send.at[t], recv_sem=ar_recv.at[t],
            device_id=device(lax.rem(k + n, chips), c), device_id_type=MESH)

    def out_copies(n, dst):
        return (
            pltpu.make_async_copy(os_.at[n, pl.ds(4 * c, 4)], dst, out_local.at[n]),
            pltpu.make_async_remote_copy(
                src_ref=os_.at[n, pl.ds(4 - 4 * c, 4)], dst_ref=dst, send_sem=out_send.at[n], recv_sem=out_recv.at[n],
                device_id=device(k, 1 - c), device_id_type=MESH),
        )

    half_cols = pl.ds(pl.multiple_of(16 * c, 16), 16)

    def out_ref(n):
        return low_hbm.at[n, :, half_cols, :]

    def native(source):
        flat = jnp.concatenate([source[:, m].reshape(64, LANES) for m in range(CHUNK)], axis=1)
        whole = lax.broadcasted_iota(jnp.int32, (64, CHUNK * LANES), 1) % LANES < HALF
        halves = [permuted(jnp.where(whole, flat, 0.0), perm[...], 1), permuted(jnp.where(whole, 0.0, flat), perm[...], 1)]
        return [half.reshape(8, 8, 512) for half in halves]

    def emit(n, source, dst):
        halves = native(source)
        for h in range(2):
            os_[n, :, 8 * h:8 * h + 8, :] = halves[h]
        for copy in out_copies(n, dst):
            copy.start()

    for block in (2, 3):
        @pl.when(block == 3 - c)
        def _():
            wait_block(block)
    wait_block(1)
    wait_block(4)
    for copy in far_copies:
        copy.start()
    prepare((1, 2, 3, 4), 0)
    factor_rows(0, 0, 16)

    def adi(t, carry):
        s = shifts[t]
        par = lax.rem(t, 2)

        @pl.when(t == 1)
        def _():
            send_halo(lambda copy: copy.start())

        def main(it, carry):
            line_group(par, it, [4 + n for n in range(16)])

            def rows(n, carry):
                off_row(par, it, 5 + it + 2 * n)
                off_row(par, it, 6 + it + 2 * n)
                return carry
            lax.fori_loop(0, 7 - it, rows, 0)
            return carry
        lax.fori_loop(0, ITERS, main, 0)

        def dots(r, sums):
            sums = list(sums)
            for m in range(CHUNK):
                v = [pb[i, r, m] for i in range(ITERS + 1)]
                sums = [old + v[i] * v[j] for old, (i, j) in zip(sums, PAIRS)]
            return tuple(sums)
        sums = lax.fori_loop(8, 16, dots, tuple(jnp.zeros((8, LANES), F32) for _ in PAIRS))
        packed = jnp.zeros((8, LANES), F32)
        for n, value in enumerate(sums):
            for half in range(2):
                part = jnp.sum(jnp.where(left, value, 0.0) if half == 0 else jnp.where(left, 0.0, value), axis=1, keepdims=True)
                packed = jnp.where(lane == 16 * half + n, part, packed)
        msg[t] = packed
        arb[t, k] = packed

        def send(n, carry):
            ar_copy(t, n).start()
            return carry
        lax.fori_loop(1, chips, send, 0)

        @pl.when(t == 0)
        def _():
            wait_block(0)
            wait_block(5)
            prepare((0, 5), 16)
            factor_rows(t, 16, 24)

        @pl.when(t == 1)
        def _():
            send_halo(lambda copy: copy.wait())
            for n, at in enumerate((0, 20)):
                gone = first if n == 0 else last
                for r in range(4):
                    pb[0, at + r] = jnp.where(gone, 0.0, hx[n, r])

        @pl.when(t < 2)
        def _():
            def outer(it, carry):
                line_group(par, it, [it + n for n in range(4)] + [20 - it + n for n in range(4)])

                @pl.when(it < ITERS - 1)
                def _():
                    def rows(n, carry):
                        off_row(par, it, it + 1 + n)
                        off_row(par, it, 19 - it + n)
                        return carry
                    lax.fori_loop(0, 4, rows, 0)
                return carry
            lax.fori_loop(0, ITERS, outer, 0)
            factor_rows(t + 1, 0, 24)

        @pl.when(t > 0)
        def _():
            emit(t - 1, us[...], out_ref(t - 1))

        pltpu.make_async_copy(arb.at[t, pl.ds(0, chips - 1)], arb.at[t, pl.ds(0, chips - 1)], ar_recv.at[t]).wait()
        total = jnp.sum(arb[t], axis=0)
        gram = {}
        for n, pair in enumerate(PAIRS):
            part = [jnp.sum(jnp.where(lane == 16 * half + n, total, 0.0), axis=1, keepdims=True) for half in range(2)]
            gram[pair] = jnp.where(left, part[0], part[1])
        y = solve_weights(gram)
        scale = jnp.sqrt(jnp.full((8, LANES), 2.0 * s, F32))

        def combine(r, carry):
            for m in range(CHUNK + 2):
                total = y[0] * zb[0, r, m]
                for it in range(1, ITERS):
                    total = total + y[it] * zb[it, r, m]
                ub[r, m] = total
            return carry
        lax.fori_loop(jnp.where(t < 2, 3, 7), jnp.where(t < 2, 21, 17), combine, 0)

        def keep(r, carry):
            for m in range(CHUNK):
                us[r, m] = scale * ub[8 + r, 1 + m]
            return carry
        lax.fori_loop(0, 8, keep, 0)

        twice = 2.0 * s

        def update(r, carry):
            slot = slot_of(r)
            for m in range(CHUNK):
                total = None
                for e in range(9):
                    term = ce[(9 + e) * CHUNK + m, pl.ds(slot, 1), :] * ub[r + e // 3 - 1, m + e % 3]
                    total = term if total is None else total + term
                pb[0, r, m] = pb[0, r, m] - twice * total
            return carry
        lax.fori_loop(jnp.where(t < 2, 4, 8), jnp.where(t < 2, 20, 16), update, 0)
        return carry

    lax.fori_loop(0, STEPS, adi, 0)

    res_at = res_hbm.at[:, half_cols, :]
    emit(STEPS - 1, us[...], out_ref(STEPS - 1))
    emit(STEPS, pb[0, 8:16], res_at)

    for copy in near_copies + far_copies:
        copy.wait_send()

    def drain(t, carry):
        pltpu.make_async_copy(arb.at[t, pl.ds(0, chips - 1)], arb.at[t, pl.ds(0, chips - 1)], ar_send.at[t]).wait()
        for copy in out_copies(t, out_ref(t)):
            copy.wait()
        return carry
    lax.fori_loop(0, STEPS, drain, 0)
    for copy in out_copies(STEPS, res_at):
        copy.wait()


def solution(mesh):
    chips = mesh.shape["rows"] // 2

    def shards(stiffness, mass, shifts, factor):
        field = (24, CHUNK, 8, LANES)
        framed = (24, CHUNK + 2, 8, LANES)
        dma = pltpu.SemaphoreType.DMA
        return pl.pallas_call(
            functools.partial(kernel, chips),
            out_shape=(jax.ShapeDtypeStruct((STEPS, 4, 32, 512), F32), jax.ShapeDtypeStruct((4, 32, 512), F32)),
            in_specs=[pl.BlockSpec(memory_space=pltpu.SMEM)] + [pl.BlockSpec(memory_space=pl.ANY)] * 3,
            out_specs=(pl.BlockSpec(memory_space=pl.ANY), pl.BlockSpec(memory_space=pl.ANY)),
            scratch_shapes=[
                pltpu.VMEM((512, CHUNK * LANES), BF16),
                pltpu.VMEM((9, 4, 512), F32),
                pltpu.VMEM((9, 4, 512), F32),
                pltpu.VMEM((4, 32, 512), F32),
                pltpu.VMEM((18 * 16, 512), F32),
                pltpu.VMEM((18 * 4, 512), F32),
                pltpu.VMEM((2, 4, CHUNK, 8, LANES), F32),
                pltpu.VMEM((6, 18 * 4, 512), F32),
                pltpu.VMEM((18 * CHUNK, 24, LANES), F32),
                pltpu.VMEM((2, COUNT, 24, LANES), F32),
                pltpu.VMEM((ITERS + 1,) + field, F32),
                pltpu.VMEM((ITERS,) + framed, F32),
                pltpu.VMEM(framed, F32),
                pltpu.VMEM((8, CHUNK, 8, LANES), F32),
                pltpu.VMEM((STEPS + 1, 8, 16, 512), F32),
                pltpu.VMEM((STEPS, chips, 8, LANES), F32),
                pltpu.VMEM((2, 4, CHUNK, 8, LANES), F32),
                pltpu.VMEM((STEPS, 8, LANES), F32),
                dma((3,)),
                dma((3, 2)),
                dma((6, 2)),
                dma((2, 2)),
                dma((STEPS,)),
                dma((STEPS,)),
                dma((2,)),
                dma((2,)),
                dma((STEPS + 1,)),
                dma((STEPS + 1,)),
                dma((STEPS + 1,)),
            ],
            compiler_params=pltpu.CompilerParams(
                collective_id=0, has_side_effects=True, vmem_limit_bytes=60 << 20),
        )(shifts, stiffness, mass, factor)

    return jax.shard_map(
        shards,
        mesh=mesh,
        in_specs=(P(None, "rows", None), P(None, "rows", None), P(), P("rows", None, None)),
        out_specs=(P(None, "rows", None, None), P("rows", None, None)),
        check_vma=False,
    )
```

```python
import functools

import jax
import jax.numpy as jnp
from jax import lax
from jax.experimental import pallas as pl
from jax.experimental.pallas import tpu as pltpu
from jax.sharding import PartitionSpec as P

STEPS = 3
ITERS = 4
MESH = pl.DeviceIdType.MESH
PAIRS = [(i, j) for i in range(ITERS + 1) for j in range(i, ITERS + 1)]
LANES = 128
CHUNK = 8
HALF = 64
F32 = jnp.float32
BF16 = jnp.bfloat16

NAMES = ["w%d" % n for n in range(1, 7)] + ["i%d" % n for n in range(7)] + ["u%d" % n for n in range(6)]
NAMES += ["e%d" % n for n in range(7)] + ["f%d" % n for n in range(7)] + ["a7", "c7", "inv"]
NAMES += ["p%d%s%d" % (level, way, reach) for level in range(3) for way in "du" for reach in (1, 2, 3)]
SLOT = {name: n for n, name in enumerate(NAMES)}
OFF = (0, 1, 2, 6, 7, 8)
COUNT = len(NAMES) + len(OFF) * CHUNK


def lane_roll(x, shift):
    return pltpu.roll(x, shift % LANES, axis=x.ndim - 1)


def split3(x):
    a = x.astype(BF16)
    rest = x - a.astype(F32)
    b = rest.astype(BF16)
    c = (rest - b.astype(F32)).astype(BF16)
    return a, b, c


def permuted(x, perm, dim=0):
    rows = x.shape[0]
    moved = lax.dot_general(jnp.concatenate(split3(x), axis=0), perm, (((1,), (dim,)), ((), ())), preferred_element_type=F32)
    return moved[:rows] + moved[rows:2 * rows] + moved[2 * rows:]


def line_factors(a, b, c):
    out = {}
    last = CHUNK - 1
    i, u, w = [], [], [None]
    for m in range(last):
        pivot = b[m]
        if m:
            w.append(a[m] * i[m - 1])
            pivot = pivot - w[m] * c[m - 1]
        i.append(1.0 / pivot)
        u.append(c[m] * i[m])
    t = [a[0]]
    for m in range(1, last):
        t.append(-w[m] * t[m - 1])
    e, f = [None] * last, [None] * last
    e[last - 1] = t[last - 1] * i[last - 1]
    f[last - 1] = u[last - 1]
    for m in reversed(range(last - 1)):
        e[m] = t[m] * i[m] - u[m] * e[m + 1]
        f[m] = -u[m] * f[m + 1]
    for m in range(last):
        out["i%d" % m], out["e%d" % m], out["f%d" % m] = i[m], e[m], f[m]
        if m:
            out["w%d" % m] = w[m]
        if m < last - 1:
            out["u%d" % m] = u[m]
    out["a7"], out["c7"] = a[last], c[last]
    low = -a[last] * e[last - 1]
    mid = b[last] - a[last] * f[last - 1] - c[last] * lane_roll(e[0], -1)
    high = -c[last] * lane_roll(f[0], -1)
    for level in range(3):
        k = 1 << (2 * level)
        pairs = []
        for reach in (k, 2 * k):
            inv = 1.0 / mid
            al = -low * lane_roll(inv, reach)
            ga = -high * lane_roll(inv, -reach)
            mid = mid + al * lane_roll(high, reach) + ga * lane_roll(low, -reach)
            low, high = al * lane_roll(low, reach), ga * lane_roll(high, -reach)
            pairs.append((al, ga))
        (al1, ga1), (al2, ga2) = pairs
        merged = {
            "d1": al1 + al2 * lane_roll(ga1, 2 * k), "d2": al2, "d3": al2 * lane_roll(al1, 2 * k),
            "u1": ga1 + ga2 * lane_roll(al1, -2 * k), "u2": ga2, "u3": ga2 * lane_roll(ga1, -2 * k),
        }
        for key, value in merged.items():
            out["p%d%s" % (level, key)] = value
    inv = 1.0 / mid
    out["inv"] = inv
    for key in ("d1", "d2", "d3", "u1", "u2", "u3"):
        out["p2" + key] = out["p2" + key] * inv
    return out


def least_squares(columns, initial):
    count = len(columns)
    cosines, sines = [], []
    rhs = [initial] + [None] * count
    upper = []
    for position in range(count):
        column = list(columns[position])
        for earlier in range(position):
            first = cosines[earlier] * column[earlier] + sines[earlier] * column[earlier + 1]
            second = -sines[earlier] * column[earlier] + cosines[earlier] * column[earlier + 1]
            column[earlier], column[earlier + 1] = first, second
        radius = jnp.sqrt(column[position] * column[position] + column[position + 1] * column[position + 1])
        inverse = 1.0 / radius
        cosine = column[position] * inverse
        sine = column[position + 1] * inverse
        cosines.append(cosine)
        sines.append(sine)
        rhs[position + 1] = -sine * rhs[position]
        rhs[position] = cosine * rhs[position]
        upper.append(column[:position] + [inverse])
    y = [None] * count
    for position in reversed(range(count)):
        accum = rhs[position]
        for onward in range(position + 1, count):
            accum = accum - upper[onward][position] * y[onward]
        y[position] = accum * upper[position][position]
    return y


def solve_weights(gram):
    n = ITERS + 1
    r = {}
    for i in range(n):
        pivot = gram[(i, i)]
        for m in range(i):
            pivot = pivot - r[(m, i)] * r[(m, i)]
        pivot = jnp.maximum(pivot, gram[(i, i)] * 1e-9)
        root = jnp.sqrt(pivot)
        r[(i, i)] = root
        inverse = 1.0 / root
        for j in range(i + 1, n):
            value = gram[(i, j)]
            for m in range(i):
                value = value - r[(m, i)] * r[(m, j)]
            r[(i, j)] = value * inverse
    columns = []
    for k in range(ITERS):
        columns.append([r[(i, k)] + r[(i, k + 1)] for i in range(k + 1)] + [r[(k + 1, k + 1)]])
    return least_squares(columns, r[(0, 0)])


def kernel(chips, shifts, stiff_hbm, mass_hbm, factor_hbm, low_hbm, res_hbm,
           perm, own_s, own_m, own_w, lhs, send_c, send_w, raw_c, ce, fc, pb, zb, ub, os_, arb, hx, msg,
           own_sem, in_send, in_recv, far_send, ar_send, ar_recv, hx_send, hx_recv, out_send, out_recv, out_local):
    me = lax.axis_index("rows")
    k = me // 2
    c = me % 2
    up = lax.rem(k + chips - 1, chips)
    down = lax.rem(k + 1, chips)

    def device(chip, core):
        return (chip * 2 + core,)

    barrier = pltpu.get_barrier_semaphore()

    def greet(n, carry):
        pl.semaphore_signal(barrier, inc=1, device_id=device(lax.rem(k + n, chips), c), device_id_type=MESH)
        return carry

    for chip in (k, up, down):
        pl.semaphore_signal(barrier, inc=1, device_id=device(chip, 1 - c), device_id_type=MESH)
    lax.fori_loop(1, chips, greet, 0)

    own_copies = [
        pltpu.make_async_copy(stiff_hbm, own_s, own_sem.at[0]),
        pltpu.make_async_copy(mass_hbm, own_m, own_sem.at[1]),
        pltpu.make_async_copy(factor_hbm, own_w, own_sem.at[2]),
    ]
    for copy in own_copies:
        copy.start()

    row = lax.broadcasted_iota(jnp.int32, (512, 512), 0)
    col = lax.broadcasted_iota(jnp.int32, (512, 512), 1)
    perm[...] = jnp.where(row == CHUNK * (col % HALF) + col // HALF, 1.0, 0.0).astype(BF16)

    lane = lax.broadcasted_iota(jnp.int32, (8, LANES), 1)
    left = lane < HALF
    lane1 = lax.broadcasted_iota(jnp.int32, (1, LANES), 1)
    left1 = lane1 < HALF
    first = k == 0
    last = k == chips - 1
    own = 2 + c

    for copy in own_copies:
        copy.wait()
    for e in range(18):
        lhs[4 * e:4 * e + 4, :] = own_s[e] if e < 9 else own_m[e - 9]
    send_c[...] = permuted(lhs[0:72, :], perm[...])
    moved = permuted(own_w[...].reshape(128, 512), perm[...])
    for core in range(2):
        for r in range(4):
            at = 32 * r + 16 * core
            for q in range(4):
                one = moved[at:at + 8, q * LANES:(q + 1) * LANES]
                two = moved[at + 8:at + 16, q * LANES:(q + 1) * LANES]
                send_w[core, r, 2 * q] = jnp.where(left, one, lane_roll(two, HALF))
                send_w[core, r, 2 * q + 1] = jnp.where(left, lane_roll(one, HALF), two)
    raw_c[own] = send_c[...]
    pb[0, pl.ds(4 * own, 4)] = send_w[c]

    pl.semaphore_wait(barrier, chips - 1 + 3)

    def block_copies(chip, core, block, sems):
        return [
            pltpu.make_async_remote_copy(
                src_ref=send_c, dst_ref=raw_c.at[block],
                send_sem=sems.at[0], recv_sem=in_recv.at[block, 0], device_id=device(chip, core), device_id_type=MESH),
            pltpu.make_async_remote_copy(
                src_ref=send_w.at[core], dst_ref=pb.at[0, pl.ds(4 * block, 4)],
                send_sem=sems.at[1], recv_sem=in_recv.at[block, 1], device_id=device(chip, core), device_id_type=MESH),
        ]

    near_chip = lax.rem(k + 2 * c - 1 + chips, chips)
    far_chip = lax.rem(k + 1 - 2 * c + chips, chips)
    near_copies = []
    for core in range(2):
        near_copies += block_copies(near_chip, core, 4 - 3 * c, in_send.at[core])
    near_copies += block_copies(k, 1 - c, own, in_send.at[2])
    far_copies = []
    for core in range(2):
        far_copies += block_copies(far_chip, core, 5 * c, far_send.at[core])
    for copy in near_copies:
        copy.start()

    def wait_block(block):
        pltpu.make_async_copy(raw_c.at[block], raw_c.at[block], in_recv.at[block, 0]).wait()
        rows = pb.at[0, pl.ds(4 * block, 4)]
        pltpu.make_async_copy(rows, rows, in_recv.at[block, 1]).wait()

    def absent(block):
        if block < 2:
            return first
        if block > 3:
            return last
        return None

    def prepare(blocks, base):
        count = 4 * len(blocks)
        for e in range(18):
            for n, block in enumerate(blocks):
                value = raw_c[block, 4 * e:4 * e + 4, :]
                gone = absent(block)
                if gone is not None:
                    value = jnp.where(gone, 1.0 if e == 4 else 0.0, value)
                lhs[e * count + 4 * n:e * count + 4 * n + 4, :] = value
        for e in range(18):
            for q in range(4):
                value = lhs[e * count:(e + 1) * count, q * LANES:(q + 1) * LANES]
                other = lane_roll(value, HALF)
                both = [jnp.where(left1, value, other), jnp.where(left1, other, value)]
                if q == 0 and e % 3 == 0:
                    both[0] = jnp.where(lane1 % HALF == 0, 0.0, both[0])
                if q == 3 and e % 3 == 2:
                    both[1] = jnp.where(lane1 % HALF == HALF - 1, 0.0, both[1])
                for n in range(2):
                    ce[e * CHUNK + 2 * q + n, base:base + count, :] = both[n]
        for block in blocks:
            gone = absent(block)
            if gone is not None:
                @pl.when(gone)
                def _():
                    pb[0, 4 * block:4 * block + 4] = jnp.zeros((4, CHUNK, 8, LANES), F32)

    def factor_rows(t, lo, hi):
        s = shifts[t]
        par = lax.rem(t, 2)

        def entry(e, m):
            return ce[e * CHUNK + m, lo:hi, :] + s * ce[(9 + e) * CHUNK + m, lo:hi, :]
        parts = line_factors(*[[entry(e, m) for m in range(CHUNK)] for e in (3, 4, 5)])
        for name, value in parts.items():
            fc[par, SLOT[name], lo:hi, :] = value
        for n, e in enumerate(OFF):
            for m in range(CHUNK):
                fc[par, len(NAMES) + n * CHUNK + m, lo:hi, :] = entry(e, m)

    def slot_of(r):
        return jnp.where(r < 4, r + 16, jnp.where(r < 20, r - 4, r))

    def line_group(par, it, rows):
        slots = [slot_of(r) for r in rows]

        def co(name, n):
            return fc[par, SLOT[name], pl.ds(slots[n], 1), :]

        g, d = [], []
        for n, r in enumerate(rows):
            v = [pb[it, r, m] for m in range(CHUNK)]
            for m in range(1, CHUNK - 1):
                v[m] = v[m] - co("w%d" % m, n) * v[m - 1]
            x = [v[m] * co("i%d" % m, n) for m in range(CHUNK - 1)]
            for m in reversed(range(CHUNK - 2)):
                x[m] = x[m] - co("u%d" % m, n) * x[m + 1]
            d.append(v[-1] - co("a7", n) * x[-1] - co("c7", n) * lane_roll(x[0], -1))
            g.append(x)
        for level in range(3):
            step = 1 << (2 * level)
            new = []
            for n, v in enumerate(d):
                total = v if level < 2 else v * co("inv", n)
                for reach in (1, 2, 3):
                    total = total + (co("p%dd%d" % (level, reach), n) * lane_roll(v, reach * step)
                                     + co("p%du%d" % (level, reach), n) * lane_roll(v, -reach * step))
                new.append(total)
            d = new
        for n, r in enumerate(rows):
            after = d[n]
            before = lane_roll(after, 1)
            zb[it, r, 0] = before
            zb[it, r, CHUNK] = after
            for m in range(CHUNK - 1):
                value = g[n][m] - co("e%d" % m, n) * before - co("f%d" % m, n) * after
                zb[it, r, m + 1] = value
                if m == 0:
                    zb[it, r, CHUNK + 1] = lane_roll(value, -1)

    def off_row(par, it, r):
        slot = slot_of(r)
        for m in range(CHUNK):
            total = None
            for n, e in enumerate(OFF):
                source = zb[it, r + (-1 if e < 3 else 1), m + e % 3]
                term = fc[par, len(NAMES) + n * CHUNK + m, pl.ds(slot, 1), :] * source
                total = term if total is None else total + term
            pb[it + 1, r, m] = total

    if chips == 64:
        ahead = [[lax.rem(lax.div(k, stride) + n, 4) * stride for n in range(4)] for stride in (16, 4, 1)]
        spans = sorted(
            ((a, b, d) for a in range(4) for b in range(4) for d in range(4) if (a, b, d) != (0, 0, 0)),
            key=lambda offset: -sum(min(n, 4 - n) for n in offset))
        others = [ahead[0][a] + ahead[1][b] + ahead[2][d] for a, b, d in spans]
    else:
        others = [lax.rem(k + n, chips) for n in range(1, chips)]

    def send_halo(do):
        for n, (chip, at) in enumerate(((down, 8), (up, 12))):
            copy = pltpu.make_async_remote_copy(
                src_ref=pb.at[0, pl.ds(at, 4)], dst_ref=hx.at[n], send_sem=hx_send.at[n], recv_sem=hx_recv.at[n],
                device_id=device(chip, c), device_id_type=MESH)
            do(copy)

    def ar_copy(t, chip):
        return pltpu.make_async_remote_copy(
            src_ref=msg.at[t], dst_ref=arb.at[t, k], send_sem=ar_send.at[t], recv_sem=ar_recv.at[t],
            device_id=device(chip, c), device_id_type=MESH)

    def out_copies(n, dst):
        return (
            pltpu.make_async_copy(os_.at[n, pl.ds(4 * c, 4)], dst, out_local.at[n]),
            pltpu.make_async_remote_copy(
                src_ref=os_.at[n, pl.ds(4 - 4 * c, 4)], dst_ref=dst, send_sem=out_send.at[n], recv_sem=out_recv.at[n],
                device_id=device(k, 1 - c), device_id_type=MESH),
        )

    half_cols = pl.ds(pl.multiple_of(16 * c, 16), 16)

    def out_ref(n):
        return low_hbm.at[n, :, half_cols, :]

    def native(source):
        whole = left[None]
        tiles = [[], []]
        for q in range(4):
            even, odd = source[:, 2 * q], source[:, 2 * q + 1]
            tiles[0].append(jnp.where(whole, even, lane_roll(odd, HALF)).reshape(64, LANES))
            tiles[1].append(jnp.where(whole, lane_roll(even, HALF), odd).reshape(64, LANES))
        flat = jnp.concatenate([jnp.concatenate(t, axis=1) for t in tiles], axis=0)
        return permuted(flat, perm[...], 1).reshape(2, 8, 8, 512)

    def emit(n, source, dst):
        halves = native(source)
        for h in range(2):
            os_[n, :, 8 * h:8 * h + 8, :] = halves[h]
        for copy in out_copies(n, dst):
            copy.start()

    def emit_low(n):
        scale = jnp.sqrt(jnp.full((1, 1, 8, LANES), 2.0 * shifts[n], F32))
        emit(n, scale * ub[8:16, 1:CHUNK + 1], out_ref(n))

    for block in (2, 3):
        @pl.when(block == 3 - c)
        def _():
            wait_block(block)
    for copy in near_copies:
        copy.wait_send()
    for copy in far_copies:
        copy.start()
    wait_block(1)
    wait_block(4)
    prepare((1, 2, 3, 4), 0)
    factor_rows(0, 0, 16)

    def adi(t, carry):
        s = shifts[t]
        par = lax.rem(t, 2)

        def main(it, carry):
            line_group(par, it, [4 + n for n in range(16)])

            def rows(n, carry):
                off_row(par, it, 5 + it + 2 * n)
                off_row(par, it, 6 + it + 2 * n)
                return carry
            lax.fori_loop(0, 7 - it, rows, 0)
            return carry
        lax.fori_loop(0, ITERS, main, 0)

        def dots(r, sums):
            sums = list(sums)
            for m in range(CHUNK):
                v = [pb[i, r, m] for i in range(ITERS + 1)]
                sums = [old + v[i] * v[j] for old, (i, j) in zip(sums, PAIRS)]
            return tuple(sums)
        sums = lax.fori_loop(8, 16, dots, tuple(jnp.zeros((8, LANES), F32) for _ in PAIRS))
        packed = jnp.zeros((8, LANES), F32)
        for n, value in enumerate(sums):
            for half in range(2):
                part = jnp.sum(jnp.where(left, value, 0.0) if half == 0 else jnp.where(left, 0.0, value), axis=1, keepdims=True)
                packed = jnp.where(lane == 16 * half + n, part, packed)
        msg[t] = packed
        arb[t, k] = packed

        for chip in others:
            ar_copy(t, chip).start()

        @pl.when(t < 2)
        def _():
            factor_rows(t + 1, 0, 16)

        @pl.when(t > 0)
        def _():
            emit_low(t - 1)

        @pl.when(t == 0)
        def _():
            wait_block(0)
            wait_block(5)
            prepare((0, 5), 16)
            factor_rows(0, 16, 24)
            factor_rows(1, 16, 24)

        @pl.when(t == 1)
        def _():
            send_halo(lambda copy: copy.wait())
            for n, at in enumerate((0, 20)):
                gone = first if n == 0 else last
                for r in range(4):
                    pb[0, at + r] = jnp.where(gone, 0.0, hx[n, r])

        @pl.when(t < 2)
        def _():
            def outer(it, carry):
                line_group(par, it, [it + n for n in range(4)] + [20 - it + n for n in range(4)])

                @pl.when(it < ITERS - 1)
                def _():
                    def rows(n, carry):
                        off_row(par, it, it + 1 + n)
                        off_row(par, it, 19 - it + n)
                        return carry
                    lax.fori_loop(0, 4, rows, 0)
                return carry
            lax.fori_loop(0, ITERS, outer, 0)

        pltpu.make_async_copy(arb.at[t, pl.ds(0, chips - 1)], arb.at[t, pl.ds(0, chips - 1)], ar_recv.at[t]).wait()
        total = jnp.sum(arb[t], axis=0)
        gram = {}
        for n, pair in enumerate(PAIRS):
            part = [jnp.sum(jnp.where(lane == 16 * half + n, total, 0.0), axis=1, keepdims=True) for half in range(2)]
            gram[pair] = jnp.where(left, part[0], part[1])
        y = solve_weights(gram)

        def combine(r, carry):
            for m in range(CHUNK + 2):
                total = y[0] * zb[0, r, m]
                for it in range(1, ITERS):
                    total = total + y[it] * zb[it, r, m]
                ub[r, m] = total
            return carry

        twice = 2.0 * s

        def update(r, carry):
            slot = slot_of(r)
            for m in range(CHUNK):
                total = None
                for e in range(9):
                    term = ce[(9 + e) * CHUNK + m, pl.ds(slot, 1), :] * ub[r + e // 3 - 1, m + e % 3]
                    total = term if total is None else total + term
                pb[0, r, m] = pb[0, r, m] - twice * total
            return carry
        lax.fori_loop(7, 17, combine, 0)
        lax.fori_loop(8, 16, update, 0)

        @pl.when(t == 0)
        def _():
            send_halo(lambda copy: copy.start())

        @pl.when(t < 2)
        def _():
            lax.fori_loop(3, 7, combine, 0)
            lax.fori_loop(17, 21, combine, 0)
            lax.fori_loop(4, 8, update, 0)
            lax.fori_loop(16, 20, update, 0)
        return carry

    lax.fori_loop(0, STEPS, adi, 0)

    res_at = res_hbm.at[:, half_cols, :]
    emit_low(STEPS - 1)
    emit(STEPS, pb[0, 8:16], res_at)

    for copy in far_copies:
        copy.wait_send()

    def drain(t, carry):
        pltpu.make_async_copy(arb.at[t, pl.ds(0, chips - 1)], arb.at[t, pl.ds(0, chips - 1)], ar_send.at[t]).wait()
        for copy in out_copies(t, out_ref(t)):
            copy.wait()
        return carry
    lax.fori_loop(0, STEPS, drain, 0)
    for copy in out_copies(STEPS, res_at):
        copy.wait()


def solution(mesh):
    chips = mesh.shape["rows"] // 2

    def shards(stiffness, mass, shifts, factor):
        field = (24, CHUNK, 8, LANES)
        framed = (24, CHUNK + 2, 8, LANES)
        dma = pltpu.SemaphoreType.DMA
        return pl.pallas_call(
            functools.partial(kernel, chips),
            out_shape=(jax.ShapeDtypeStruct((STEPS, 4, 32, 512), F32), jax.ShapeDtypeStruct((4, 32, 512), F32)),
            in_specs=[pl.BlockSpec(memory_space=pltpu.SMEM)] + [pl.BlockSpec(memory_space=pl.ANY)] * 3,
            out_specs=(pl.BlockSpec(memory_space=pl.ANY), pl.BlockSpec(memory_space=pl.ANY)),
            scratch_shapes=[
                pltpu.VMEM((512, 512), BF16),
                pltpu.VMEM((9, 4, 512), F32),
                pltpu.VMEM((9, 4, 512), F32),
                pltpu.VMEM((4, 32, 512), F32),
                pltpu.VMEM((18 * 16, 512), F32),
                pltpu.VMEM((18 * 4, 512), F32),
                pltpu.VMEM((2, 4, CHUNK, 8, LANES), F32),
                pltpu.VMEM((6, 18 * 4, 512), F32),
                pltpu.VMEM((18 * CHUNK, 24, LANES), F32),
                pltpu.VMEM((2, COUNT, 24, LANES), F32),
                pltpu.VMEM((ITERS + 1,) + field, F32),
                pltpu.VMEM((ITERS,) + framed, F32),
                pltpu.VMEM(framed, F32),
                pltpu.VMEM((STEPS + 1, 8, 16, 512), F32),
                pltpu.VMEM((STEPS, chips, 8, LANES), F32),
                pltpu.VMEM((2, 4, CHUNK, 8, LANES), F32),
                pltpu.VMEM((STEPS, 8, LANES), F32),
                dma((3,)),
                dma((3, 2)),
                dma((6, 2)),
                dma((2, 2)),
                dma((STEPS,)),
                dma((STEPS,)),
                dma((2,)),
                dma((2,)),
                dma((STEPS + 1,)),
                dma((STEPS + 1,)),
                dma((STEPS + 1,)),
            ],
            compiler_params=pltpu.CompilerParams(
                collective_id=0, has_side_effects=True, vmem_limit_bytes=60 << 20),
        )(shifts, stiffness, mass, factor)

    return jax.shard_map(
        shards,
        mesh=mesh,
        in_specs=(P(None, "rows", None), P(None, "rows", None), P(), P("rows", None, None)),
        out_specs=(P(None, "rows", None, None), P("rows", None, None)),
        check_vma=False,
    )
```

```python
import functools

import jax
import jax.numpy as jnp
from jax import lax
from jax.experimental import pallas as pl
from jax.experimental.pallas import tpu as pltpu
from jax.sharding import PartitionSpec as P

STEPS = 3
ITERS = 4
MESH = pl.DeviceIdType.MESH
PAIRS = [(i, j) for i in range(ITERS + 1) for j in range(i, ITERS + 1)]
LANES = 128
CHUNK = 8
HALF = 64
F32 = jnp.float32
BF16 = jnp.bfloat16

NAMES = ["w%d" % n for n in range(1, 7)] + ["i%d" % n for n in range(7)] + ["u%d" % n for n in range(6)]
NAMES += ["e%d" % n for n in range(7)] + ["f%d" % n for n in range(7)] + ["a7", "c7", "inv", "en", "fn"]
NAMES += ["p%d%s%d" % (level, way, reach) for level in range(3) for way in "du" for reach in (1, 2, 3)]
SLOT = {name: n for n, name in enumerate(NAMES)}
OFF = (0, 1, 2, 6, 7, 8)
COUNT = len(NAMES) + len(OFF) * CHUNK


def lane_roll(x, shift):
    return pltpu.roll(x, shift % LANES, axis=x.ndim - 1)


def split3(x):
    a = x.astype(BF16)
    rest = x - a.astype(F32)
    b = rest.astype(BF16)
    c = (rest - b.astype(F32)).astype(BF16)
    return a, b, c


def permuted(x, perm, dim=0):
    rows = x.shape[0]
    moved = lax.dot_general(jnp.concatenate(split3(x), axis=0), perm, (((1,), (dim,)), ((), ())), preferred_element_type=F32)
    return moved[:rows] + moved[rows:2 * rows] + moved[2 * rows:]


def line_factors(a, b, c):
    out = {}
    last = CHUNK - 1
    i, u, w = [], [], [None]
    for m in range(last):
        pivot = b[m]
        if m:
            w.append(a[m] * i[m - 1])
            pivot = pivot - w[m] * c[m - 1]
        i.append(1.0 / pivot)
        u.append(c[m] * i[m])
    t = [a[0]]
    for m in range(1, last):
        t.append(-w[m] * t[m - 1])
    e, f = [None] * last, [None] * last
    e[last - 1] = t[last - 1] * i[last - 1]
    f[last - 1] = u[last - 1]
    for m in reversed(range(last - 1)):
        e[m] = t[m] * i[m] - u[m] * e[m + 1]
        f[m] = -u[m] * f[m + 1]
    for m in range(last):
        out["i%d" % m], out["e%d" % m], out["f%d" % m] = i[m], e[m], f[m]
        if m:
            out["w%d" % m] = w[m]
        if m < last - 1:
            out["u%d" % m] = u[m]
    out["a7"], out["c7"] = a[last], c[last]
    out["en"], out["fn"] = lane_roll(e[0], -1), lane_roll(f[0], -1)
    low = -a[last] * e[last - 1]
    mid = b[last] - a[last] * f[last - 1] - c[last] * out["en"]
    high = -c[last] * out["fn"]
    for level in range(3):
        k = 1 << (2 * level)
        pairs = []
        for reach in (k, 2 * k):
            inv = 1.0 / mid
            al = -low * lane_roll(inv, reach)
            ga = -high * lane_roll(inv, -reach)
            mid = mid + al * lane_roll(high, reach) + ga * lane_roll(low, -reach)
            low, high = al * lane_roll(low, reach), ga * lane_roll(high, -reach)
            pairs.append((al, ga))
        (al1, ga1), (al2, ga2) = pairs
        merged = {
            "d1": al1 + al2 * lane_roll(ga1, 2 * k), "d2": al2, "d3": al2 * lane_roll(al1, 2 * k),
            "u1": ga1 + ga2 * lane_roll(al1, -2 * k), "u2": ga2, "u3": ga2 * lane_roll(ga1, -2 * k),
        }
        for key, value in merged.items():
            out["p%d%s" % (level, key)] = value
    inv = 1.0 / mid
    out["inv"] = inv
    for key in ("d1", "d2", "d3", "u1", "u2", "u3"):
        out["p2" + key] = out["p2" + key] * inv
    return out


def least_squares(columns, initial):
    count = len(columns)
    cosines, sines = [], []
    rhs = [initial] + [None] * count
    upper = []
    for position in range(count):
        column = list(columns[position])
        for earlier in range(position):
            first = cosines[earlier] * column[earlier] + sines[earlier] * column[earlier + 1]
            second = -sines[earlier] * column[earlier] + cosines[earlier] * column[earlier + 1]
            column[earlier], column[earlier + 1] = first, second
        radius = jnp.sqrt(column[position] * column[position] + column[position + 1] * column[position + 1])
        inverse = 1.0 / radius
        cosine = column[position] * inverse
        sine = column[position + 1] * inverse
        cosines.append(cosine)
        sines.append(sine)
        rhs[position + 1] = -sine * rhs[position]
        rhs[position] = cosine * rhs[position]
        upper.append(column[:position] + [inverse])
    y = [None] * count
    for position in reversed(range(count)):
        accum = rhs[position]
        for onward in range(position + 1, count):
            accum = accum - upper[onward][position] * y[onward]
        y[position] = accum * upper[position][position]
    return y


def solve_weights(gram):
    n = ITERS + 1
    r = {}
    for i in range(n):
        pivot = gram[(i, i)]
        for m in range(i):
            pivot = pivot - r[(m, i)] * r[(m, i)]
        pivot = jnp.maximum(pivot, gram[(i, i)] * 1e-9)
        root = jnp.sqrt(pivot)
        r[(i, i)] = root
        inverse = 1.0 / root
        for j in range(i + 1, n):
            value = gram[(i, j)]
            for m in range(i):
                value = value - r[(m, i)] * r[(m, j)]
            r[(i, j)] = value * inverse
    columns = []
    for k in range(ITERS):
        columns.append([r[(i, k)] + r[(i, k + 1)] for i in range(k + 1)] + [r[(k + 1, k + 1)]])
    return least_squares(columns, r[(0, 0)])


def kernel(chips, shifts_hbm, stiff_hbm, mass_hbm, factor_hbm, low_hbm, res_hbm,
           perm, own_s, own_m, own_w, lhs, send_c, send_w, raw_c, ce, fc, pb, zb, ub, os_, arb, hx, msg, shifts,
           own_sem, in_send, in_recv, far_send, ar_send, ar_recv, hx_send, hx_recv, out_send, out_recv, out_local):
    me = lax.axis_index("rows")
    k = me // 2
    c = me % 2
    up = lax.rem(k + chips - 1, chips)
    down = lax.rem(k + 1, chips)

    def device(chip, core):
        return (chip * 2 + core,)

    barrier = pltpu.get_barrier_semaphore()

    if chips == 64:
        ahead = [[lax.rem(lax.div(k, stride) + n, 4) * stride for n in range(4)] for stride in (16, 4, 1)]
        spans = sorted(
            ((a, b, d) for a in range(4) for b in range(4) for d in range(4) if (a, b, d) != (0, 0, 0)),
            key=lambda offset: -sum(min(n, 4 - n) for n in offset))
        others = [ahead[0][a] + ahead[1][b] + ahead[2][d] for a, b, d in spans]
    else:
        others = [lax.rem(k + n, chips) for n in range(1, chips)]

    for chip in (up, down, k):
        pl.semaphore_signal(barrier, inc=1, device_id=device(chip, 1 - c), device_id_type=MESH)
    for chip in others:
        pl.semaphore_signal(barrier, inc=1, device_id=device(chip, c), device_id_type=MESH)

    own_copies = [
        pltpu.make_async_copy(stiff_hbm, own_s, own_sem.at[0]),
        pltpu.make_async_copy(mass_hbm, own_m, own_sem.at[1]),
        pltpu.make_async_copy(factor_hbm, own_w, own_sem.at[2]),
        pltpu.make_async_copy(shifts_hbm, shifts, own_sem.at[3]),
    ]
    for copy in own_copies:
        copy.start()

    row = lax.broadcasted_iota(jnp.int32, (512, 512), 0)
    col = lax.broadcasted_iota(jnp.int32, (512, 512), 1)
    perm[...] = jnp.where(row == CHUNK * (col % HALF) + col // HALF, 1.0, 0.0).astype(BF16)

    lane = lax.broadcasted_iota(jnp.int32, (8, LANES), 1)
    left = lane < HALF
    sub = lax.broadcasted_iota(jnp.int32, (8, LANES), 0)
    halves8 = jnp.where((sub % 2 == 0) == left, 1.0, 0.0).astype(BF16)
    sub16 = lax.broadcasted_iota(jnp.int32, (16, LANES), 0)
    lane16 = lax.broadcasted_iota(jnp.int32, (16, LANES), 1)
    halves16 = jnp.where(sub16 == lane16 // HALF, 1.0, 0.0).astype(BF16)
    lane1 = lax.broadcasted_iota(jnp.int32, (1, LANES), 1)
    left1 = lane1 < HALF
    first = k == 0
    last = k == chips - 1
    own = 2 + c

    for copy in own_copies:
        copy.wait()
    for e in range(18):
        lhs[4 * e:4 * e + 4, :] = own_s[e] if e < 9 else own_m[e - 9]
    send_c[...] = permuted(lhs[0:72, :], perm[...])
    moved = permuted(own_w[...].reshape(128, 512), perm[...])
    for core in range(2):
        for r in range(4):
            at = 32 * r + 16 * core
            for q in range(4):
                one = moved[at:at + 8, q * LANES:(q + 1) * LANES]
                two = moved[at + 8:at + 16, q * LANES:(q + 1) * LANES]
                send_w[core, r, 2 * q] = jnp.where(left, one, lane_roll(two, HALF))
                send_w[core, r, 2 * q + 1] = jnp.where(left, lane_roll(one, HALF), two)
    raw_c[own] = send_c[...]
    pb[0, pl.ds(4 * own, 4)] = send_w[c]

    pl.semaphore_wait(barrier, chips - 1 + 3)

    def block_copies(chip, core, block, sems):
        return [
            pltpu.make_async_remote_copy(
                src_ref=send_c, dst_ref=raw_c.at[block],
                send_sem=sems.at[0], recv_sem=in_recv.at[block, 0], device_id=device(chip, core), device_id_type=MESH),
            pltpu.make_async_remote_copy(
                src_ref=send_w.at[core], dst_ref=pb.at[0, pl.ds(4 * block, 4)],
                send_sem=sems.at[1], recv_sem=in_recv.at[block, 1], device_id=device(chip, core), device_id_type=MESH),
        ]

    near_chip = lax.rem(k + 2 * c - 1 + chips, chips)
    far_chip = lax.rem(k + 1 - 2 * c + chips, chips)
    near_copies, far_copies = [], []
    for core in range(2):
        near_copies.append(block_copies(near_chip, core, 4 - 3 * c, in_send.at[core]))
        far_copies += block_copies(far_chip, core, 5 * c, far_send.at[core])
    near_copies.append(block_copies(k, 1 - c, own, in_send.at[2]))
    near_copies = [pair[0] for pair in near_copies] + [pair[1] for pair in near_copies]
    for copy in near_copies:
        copy.start()

    def wait_stencil(block):
        pltpu.make_async_copy(raw_c.at[block], raw_c.at[block], in_recv.at[block, 0]).wait()

    def wait_field(block):
        rows = pb.at[0, pl.ds(4 * block, 4)]
        pltpu.make_async_copy(rows, rows, in_recv.at[block, 1]).wait()

    def absent(block):
        if block < 2:
            return first
        if block > 3:
            return last
        return None

    def prepare(blocks, base):
        count = 4 * len(blocks)
        for e in range(18):
            for n, block in enumerate(blocks):
                value = raw_c[block, 4 * e:4 * e + 4, :]
                gone = absent(block)
                if gone is not None:
                    value = jnp.where(gone, 1.0 if e == 4 else 0.0, value)
                lhs[e * count + 4 * n:e * count + 4 * n + 4, :] = value
        for e in range(18):
            for q in range(4):
                value = lhs[e * count:(e + 1) * count, q * LANES:(q + 1) * LANES]
                other = lane_roll(value, HALF)
                both = [jnp.where(left1, value, other), jnp.where(left1, other, value)]
                if q == 0 and e % 3 == 0:
                    both[0] = jnp.where(lane1 % HALF == 0, 0.0, both[0])
                if q == 3 and e % 3 == 2:
                    both[1] = jnp.where(lane1 % HALF == HALF - 1, 0.0, both[1])
                for n in range(2):
                    ce[e * CHUNK + 2 * q + n, base:base + count, :] = both[n]

    def clear(block):
        @pl.when(absent(block))
        def _():
            pb[0, 4 * block:4 * block + 4] = jnp.zeros((4, CHUNK, 8, LANES), F32)

    def factor_rows(t, lo, hi):
        s = shifts[t]
        par = lax.rem(t, 2)

        def entry(e, m):
            return ce[e * CHUNK + m, lo:hi, :] + s * ce[(9 + e) * CHUNK + m, lo:hi, :]
        parts = line_factors(*[[entry(e, m) for m in range(CHUNK)] for e in (3, 4, 5)])
        for name, value in parts.items():
            fc[par, SLOT[name], lo:hi, :] = value
        for n, e in enumerate(OFF):
            for m in range(CHUNK):
                fc[par, len(NAMES) + n * CHUNK + m, lo:hi, :] = entry(e, m)

    def slot_of(r):
        return jnp.where(r < 4, r + 16, jnp.where(r < 20, r - 4, r))

    def line_group(par, it, rows):
        slots = [slot_of(r) for r in rows]

        def co(name, n):
            return fc[par, SLOT[name], pl.ds(slots[n], 1), :]

        g, d, ahead_g = [], [], []
        for n, r in enumerate(rows):
            v = [pb[it, r, m] for m in range(CHUNK)]
            for m in range(1, CHUNK - 1):
                v[m] = v[m] - co("w%d" % m, n) * v[m - 1]
            x = [v[m] * co("i%d" % m, n) for m in range(CHUNK - 1)]
            for m in reversed(range(CHUNK - 2)):
                x[m] = x[m] - co("u%d" % m, n) * x[m + 1]
            ahead_g.append(lane_roll(x[0], -1))
            d.append(v[-1] - co("a7", n) * x[-1] - co("c7", n) * ahead_g[-1])
            g.append(x)
        for level in range(3):
            step = 1 << (2 * level)
            new = []
            for n, v in enumerate(d):
                total = v if level < 2 else v * co("inv", n)
                for reach in (1, 2, 3):
                    total = total + (co("p%dd%d" % (level, reach), n) * lane_roll(v, reach * step)
                                     + co("p%du%d" % (level, reach), n) * lane_roll(v, -reach * step))
                new.append(total)
            d = new
        for n, r in enumerate(rows):
            after = d[n]
            before = lane_roll(after, 1)
            zb[it, r, 0] = before
            zb[it, r, CHUNK] = after
            for m in range(CHUNK - 1):
                zb[it, r, m + 1] = g[n][m] - co("e%d" % m, n) * before - co("f%d" % m, n) * after
            zb[it, r, CHUNK + 1] = ahead_g[n] - co("en", n) * after - co("fn", n) * lane_roll(after, -1)

    def off_row(par, it, r):
        slot = slot_of(r)
        for m in range(CHUNK):
            total = None
            for n, e in enumerate(OFF):
                source = zb[it, r + (-1 if e < 3 else 1), m + e % 3]
                term = fc[par, len(NAMES) + n * CHUNK + m, pl.ds(slot, 1), :] * source
                total = term if total is None else total + term
            pb[it + 1, r, m] = total

    def send_halo(do):
        for n, (chip, at) in enumerate(((down, 8), (up, 12))):
            copy = pltpu.make_async_remote_copy(
                src_ref=pb.at[0, pl.ds(at, 4)], dst_ref=hx.at[n], send_sem=hx_send.at[n], recv_sem=hx_recv.at[n],
                device_id=device(chip, c), device_id_type=MESH)
            do(copy)

    def ar_copy(t, chip):
        return pltpu.make_async_remote_copy(
            src_ref=msg.at[t], dst_ref=arb.at[t, k], send_sem=ar_send.at[t], recv_sem=ar_recv.at[t],
            device_id=device(chip, c), device_id_type=MESH)

    def out_copies(n, dst):
        return (
            pltpu.make_async_copy(os_.at[n, pl.ds(4 * c, 4)], dst, out_local.at[n]),
            pltpu.make_async_remote_copy(
                src_ref=os_.at[n, pl.ds(4 - 4 * c, 4)], dst_ref=dst, send_sem=out_send.at[n], recv_sem=out_recv.at[n],
                device_id=device(k, 1 - c), device_id_type=MESH),
        )

    half_cols = pl.ds(pl.multiple_of(16 * c, 16), 16)

    def out_ref(n):
        return low_hbm.at[n, :, half_cols, :]

    def native(source):
        whole = left[None]
        tiles = [[], []]
        for q in range(4):
            even, odd = source[:, 2 * q], source[:, 2 * q + 1]
            tiles[0].append(jnp.where(whole, even, lane_roll(odd, HALF)).reshape(64, LANES))
            tiles[1].append(jnp.where(whole, lane_roll(even, HALF), odd).reshape(64, LANES))
        flat = jnp.concatenate([jnp.concatenate(t, axis=1) for t in tiles], axis=0)
        return permuted(flat, perm[...], 1).reshape(2, 8, 8, 512)

    def emit(n, source, dst):
        halves = native(source)
        for h in range(2):
            os_[n, :, 8 * h:8 * h + 8, :] = halves[h]
        for copy in out_copies(n, dst):
            copy.start()

    def emit_low(n):
        scale = jnp.sqrt(jnp.full((1, 1, 8, LANES), 2.0 * shifts[n], F32))
        emit(n, scale * ub[8:16, 1:CHUNK + 1], out_ref(n))

    for block in (2, 3):
        @pl.when(block == 3 - c)
        def _():
            wait_stencil(block)
    wait_stencil(1)
    wait_stencil(4)
    prepare((1, 2, 3, 4), 0)
    factor_rows(0, 0, 16)
    for copy in near_copies:
        copy.wait_send()
    for copy in far_copies:
        copy.start()
    for block in (2, 3):
        @pl.when(block == 3 - c)
        def _():
            wait_field(block)
    for block in (1, 4):
        wait_field(block)
        clear(block)

    def adi(t, carry):
        s = shifts[t]
        par = lax.rem(t, 2)

        sums = {pair: jnp.zeros((8, LANES), F32) for pair in PAIRS}

        def dots(latest):
            for r in range(8, 16):
                for m in range(CHUNK):
                    newest = pb[latest, r, m]
                    for i in range(latest + 1):
                        sums[(i, latest)] = sums[(i, latest)] + newest * (newest if i == latest else pb[i, r, m])

        for it in range(ITERS):
            line_group(par, it, list(range(4 + it, 20 - it)))
            dots(it)

            def rows(n, carry):
                off_row(par, it, 5 + it + 2 * n)
                off_row(par, it, 6 + it + 2 * n)
                return carry
            lax.fori_loop(0, 7 - it, rows, 0)
        dots(ITERS)
        stacked = jnp.concatenate([sums[pair] for pair in PAIRS] + [jnp.zeros((8, LANES), F32)], axis=0)
        packed = lax.dot_general(halves16, jnp.concatenate(split3(stacked), axis=0), (((1,), (1,)), ((), ())), preferred_element_type=F32)
        packed = packed[0:2, 0:LANES] + packed[0:2, LANES:2 * LANES] + packed[0:2, 2 * LANES:]
        msg[t] = packed
        arb[t, k] = packed

        for chip in others:
            ar_copy(t, chip).start()

        @pl.when(t < 2)
        def _():
            factor_rows(t + 1, 0, 16)

        @pl.when(t > 0)
        def _():
            emit_low(t - 1)

        @pl.when(t == 0)
        def _():
            for block in (0, 5):
                wait_stencil(block)
            prepare((0, 5), 16)
            factor_rows(0, 16, 24)
            factor_rows(1, 16, 24)
            for block in (0, 5):
                wait_field(block)
                clear(block)

        @pl.when(t == 1)
        def _():
            send_halo(lambda copy: copy.wait())
            for n, at in enumerate((0, 20)):
                gone = first if n == 0 else last
                for r in range(4):
                    pb[0, at + r] = jnp.where(gone, 0.0, hx[n, r])

        @pl.when(t < 2)
        def _():
            def outer(it, carry):
                line_group(par, it, [it + n for n in range(4)] + [20 - it + n for n in range(4)])

                @pl.when(it < ITERS - 1)
                def _():
                    def rows(n, carry):
                        off_row(par, it, it + 1 + n)
                        off_row(par, it, 19 - it + n)
                        return carry
                    lax.fori_loop(0, 4, rows, 0)
                return carry
            lax.fori_loop(0, ITERS, outer, 0)

        pltpu.make_async_copy(arb.at[t, pl.ds(0, chips - 1)], arb.at[t, pl.ds(0, chips - 1)], ar_recv.at[t]).wait()
        total = jnp.sum(arb[t], axis=0)
        total = jnp.concatenate([total] * 3 + [jnp.zeros((2, LANES), F32)], axis=0)
        one, two, three = [part.astype(F32) for part in split3(total)]
        total = jnp.where(sub < 2, one, jnp.where(sub < 4, two, three)).astype(BF16)
        spread_out = lax.dot_general(total, halves8, (((0,), (0,)), ((), ())), preferred_element_type=F32)
        gram = {pair: spread_out[8 * n:8 * n + 8] for n, pair in enumerate(PAIRS)}
        y = solve_weights(gram)

        def combine(r, carry):
            for m in range(CHUNK + 2):
                total = y[0] * zb[0, r, m]
                for it in range(1, ITERS):
                    total = total + y[it] * zb[it, r, m]
                ub[r, m] = total
            return carry

        twice = 2.0 * s

        def update(r, carry):
            slot = slot_of(r)
            for m in range(CHUNK):
                total = None
                for e in range(9):
                    term = ce[(9 + e) * CHUNK + m, pl.ds(slot, 1), :] * ub[r + e // 3 - 1, m + e % 3]
                    total = term if total is None else total + term
                pb[0, r, m] = pb[0, r, m] - twice * total
            return carry
        lax.fori_loop(7, 17, combine, 0, unroll=2)
        lax.fori_loop(8, 16, update, 0, unroll=2)

        @pl.when(t == 0)
        def _():
            send_halo(lambda copy: copy.start())

        @pl.when(t < 2)
        def _():
            lax.fori_loop(3, 7, combine, 0)
            lax.fori_loop(17, 21, combine, 0)
            lax.fori_loop(4, 8, update, 0, unroll=2)
            lax.fori_loop(16, 20, update, 0, unroll=2)
        return carry

    lax.fori_loop(0, STEPS, adi, 0)

    res_at = res_hbm.at[:, half_cols, :]
    emit_low(STEPS - 1)
    emit(STEPS, pb[0, 8:16], res_at)

    for copy in far_copies:
        copy.wait_send()

    def drain(t, carry):
        pltpu.make_async_copy(arb.at[t, pl.ds(0, chips - 1)], arb.at[t, pl.ds(0, chips - 1)], ar_send.at[t]).wait()
        for copy in out_copies(t, out_ref(t)):
            copy.wait()
        return carry
    lax.fori_loop(0, STEPS, drain, 0)
    for copy in out_copies(STEPS, res_at):
        copy.wait()


def solution(mesh):
    chips = mesh.shape["rows"] // 2

    def shards(stiffness, mass, shifts, factor):
        field = (24, CHUNK, 8, LANES)
        framed = (24, CHUNK + 2, 8, LANES)
        dma = pltpu.SemaphoreType.DMA
        return pl.pallas_call(
            functools.partial(kernel, chips),
            out_shape=(jax.ShapeDtypeStruct((STEPS, 4, 32, 512), F32), jax.ShapeDtypeStruct((4, 32, 512), F32)),
            in_specs=[pl.BlockSpec(memory_space=pl.ANY)] * 4,
            out_specs=(pl.BlockSpec(memory_space=pl.ANY), pl.BlockSpec(memory_space=pl.ANY)),
            scratch_shapes=[
                pltpu.VMEM((512, 512), BF16),
                pltpu.VMEM((9, 4, 512), F32),
                pltpu.VMEM((9, 4, 512), F32),
                pltpu.VMEM((4, 32, 512), F32),
                pltpu.VMEM((18 * 16, 512), F32),
                pltpu.VMEM((18 * 4, 512), F32),
                pltpu.VMEM((2, 4, CHUNK, 8, LANES), F32),
                pltpu.VMEM((6, 18 * 4, 512), F32),
                pltpu.VMEM((18 * CHUNK, 24, LANES), F32),
                pltpu.VMEM((2, COUNT, 24, LANES), F32),
                pltpu.VMEM((ITERS + 1,) + field, F32),
                pltpu.VMEM((ITERS,) + framed, F32),
                pltpu.VMEM(framed, F32),
                pltpu.VMEM((STEPS + 1, 8, 16, 512), F32),
                pltpu.VMEM((STEPS, chips, 2, LANES), F32),
                pltpu.VMEM((2, 4, CHUNK, 8, LANES), F32),
                pltpu.VMEM((STEPS, 2, LANES), F32),
                pltpu.SMEM((STEPS,), F32),
                dma((4,)),
                dma((3, 2)),
                dma((6, 2)),
                dma((2, 2)),
                dma((STEPS,)),
                dma((STEPS,)),
                dma((2,)),
                dma((2,)),
                dma((STEPS + 1,)),
                dma((STEPS + 1,)),
                dma((STEPS + 1,)),
            ],
            compiler_params=pltpu.CompilerParams(
                collective_id=0, has_side_effects=True, vmem_limit_bytes=60 << 20),
        )(shifts, stiffness, mass, factor)

    return jax.shard_map(
        shards,
        mesh=mesh,
        in_specs=(P(None, "rows", None), P(None, "rows", None), P(), P("rows", None, None)),
        out_specs=(P(None, "rows", None, None), P("rows", None, None)),
        check_vma=False,
    )
```

```python
import functools

import jax
import jax.numpy as jnp
from jax import lax
from jax.experimental import pallas as pl
from jax.experimental.pallas import tpu as pltpu
from jax.sharding import PartitionSpec as P

STEPS = 3
ITERS = 4
MESH = pl.DeviceIdType.MESH
PAIRS = [(i, j) for i in range(ITERS + 1) for j in range(i, ITERS + 1)]
LANES = 128
CHUNK = 8
HALF = 64
F32 = jnp.float32
BF16 = jnp.bfloat16

NAMES = ["w%d" % n for n in range(1, 7)] + ["i%d" % n for n in range(7)] + ["u%d" % n for n in range(6)]
NAMES += ["e%d" % n for n in range(7)] + ["f%d" % n for n in range(7)] + ["a7", "c7", "inv", "en", "fn"]
NAMES += ["p%d%s%d" % (level, way, reach) for level in range(3) for way in "du" for reach in (1, 2, 3)]
SLOT = {name: n for n, name in enumerate(NAMES)}
OFF = (0, 1, 2, 6, 7, 8)
COUNT = len(NAMES) + len(OFF) * CHUNK


def lane_roll(x, shift):
    return pltpu.roll(x, shift % LANES, axis=x.ndim - 1)


def split3(x):
    a = x.astype(BF16)
    rest = x - a.astype(F32)
    b = rest.astype(BF16)
    c = (rest - b.astype(F32)).astype(BF16)
    return a, b, c


def permuted(x, perm, dim=0):
    rows = x.shape[0]
    moved = lax.dot_general(jnp.concatenate(split3(x), axis=0), perm, (((1,), (dim,)), ((), ())), preferred_element_type=F32)
    return moved[:rows] + moved[rows:2 * rows] + moved[2 * rows:]


def line_factors(a, b, c):
    out = {}
    last = CHUNK - 1
    i, u, w = [], [], [None]
    for m in range(last):
        pivot = b[m]
        if m:
            w.append(a[m] * i[m - 1])
            pivot = pivot - w[m] * c[m - 1]
        i.append(1.0 / pivot)
        u.append(c[m] * i[m])
    t = [a[0]]
    for m in range(1, last):
        t.append(-w[m] * t[m - 1])
    e, f = [None] * last, [None] * last
    e[last - 1] = t[last - 1] * i[last - 1]
    f[last - 1] = u[last - 1]
    for m in reversed(range(last - 1)):
        e[m] = t[m] * i[m] - u[m] * e[m + 1]
        f[m] = -u[m] * f[m + 1]
    for m in range(last):
        out["i%d" % m], out["e%d" % m], out["f%d" % m] = i[m], e[m], f[m]
        if m:
            out["w%d" % m] = w[m]
        if m < last - 1:
            out["u%d" % m] = u[m]
    out["a7"], out["c7"] = a[last], c[last]
    out["en"], out["fn"] = lane_roll(e[0], -1), lane_roll(f[0], -1)
    low = -a[last] * e[last - 1]
    mid = b[last] - a[last] * f[last - 1] - c[last] * out["en"]
    high = -c[last] * out["fn"]
    for level in range(3):
        k = 1 << (2 * level)
        pairs = []
        for reach in (k, 2 * k):
            inv = 1.0 / mid
            al = -low * lane_roll(inv, reach)
            ga = -high * lane_roll(inv, -reach)
            mid = mid + al * lane_roll(high, reach) + ga * lane_roll(low, -reach)
            low, high = al * lane_roll(low, reach), ga * lane_roll(high, -reach)
            pairs.append((al, ga))
        (al1, ga1), (al2, ga2) = pairs
        merged = {
            "d1": al1 + al2 * lane_roll(ga1, 2 * k), "d2": al2, "d3": al2 * lane_roll(al1, 2 * k),
            "u1": ga1 + ga2 * lane_roll(al1, -2 * k), "u2": ga2, "u3": ga2 * lane_roll(ga1, -2 * k),
        }
        for key, value in merged.items():
            out["p%d%s" % (level, key)] = value
    inv = 1.0 / mid
    out["inv"] = inv
    for key in ("d1", "d2", "d3", "u1", "u2", "u3"):
        out["p2" + key] = out["p2" + key] * inv
    return out


def least_squares(columns, initial):
    count = len(columns)
    cosines, sines = [], []
    rhs = [initial] + [None] * count
    upper = []
    for position in range(count):
        column = list(columns[position])
        for earlier in range(position):
            first = cosines[earlier] * column[earlier] + sines[earlier] * column[earlier + 1]
            second = -sines[earlier] * column[earlier] + cosines[earlier] * column[earlier + 1]
            column[earlier], column[earlier + 1] = first, second
        radius = jnp.sqrt(column[position] * column[position] + column[position + 1] * column[position + 1])
        inverse = 1.0 / radius
        cosine = column[position] * inverse
        sine = column[position + 1] * inverse
        cosines.append(cosine)
        sines.append(sine)
        rhs[position + 1] = -sine * rhs[position]
        rhs[position] = cosine * rhs[position]
        upper.append(column[:position] + [inverse])
    y = [None] * count
    for position in reversed(range(count)):
        accum = rhs[position]
        for onward in range(position + 1, count):
            accum = accum - upper[onward][position] * y[onward]
        y[position] = accum * upper[position][position]
    return y


def solve_weights(gram):
    n = ITERS + 1
    r = {}
    for i in range(n):
        pivot = gram[(i, i)]
        for m in range(i):
            pivot = pivot - r[(m, i)] * r[(m, i)]
        pivot = jnp.maximum(pivot, gram[(i, i)] * 1e-9)
        root = jnp.sqrt(pivot)
        r[(i, i)] = root
        inverse = 1.0 / root
        for j in range(i + 1, n):
            value = gram[(i, j)]
            for m in range(i):
                value = value - r[(m, i)] * r[(m, j)]
            r[(i, j)] = value * inverse
    columns = []
    for k in range(ITERS):
        columns.append([r[(i, k)] + r[(i, k + 1)] for i in range(k + 1)] + [r[(k + 1, k + 1)]])
    return least_squares(columns, r[(0, 0)])


def kernel(chips, shifts_hbm, stiff_hbm, mass_hbm, factor_hbm, low_hbm, res_hbm,
           perm, own_s, own_m, own_w, lhs, send_c, send_w, raw_c, ce, fc, pb, zb, ub, mz, os_, arb, hx, msg, shifts,
           own_sem, hand_send, in_send, in_recv, far_send, ar_send, ar_recv, hx_send, hx_recv, out_send, out_recv, out_local):
    me = lax.axis_index("rows")
    k = me // 2
    c = me % 2
    up = lax.rem(k + chips - 1, chips)
    down = lax.rem(k + 1, chips)

    def device(chip, core):
        return (chip * 2 + core,)

    barrier = pltpu.get_barrier_semaphore()

    if chips == 64:
        ahead = [[lax.rem(lax.div(k, stride) + n, 4) * stride for n in range(4)] for stride in (16, 4, 1)]
        spans = sorted(
            ((a, b, d) for a in range(4) for b in range(4) for d in range(4) if (a, b, d) != (0, 0, 0)),
            key=lambda offset: -sum(min(n, 4 - n) for n in offset))
        others = [ahead[0][a] + ahead[1][b] + ahead[2][d] for a, b, d in spans]
    else:
        others = [lax.rem(k + n, chips) for n in range(1, chips)]

    for chip in (up, down, k):
        pl.semaphore_signal(barrier, inc=1, device_id=device(chip, 1 - c), device_id_type=MESH)
    for chip in others:
        pl.semaphore_signal(barrier, inc=1, device_id=device(chip, c), device_id_type=MESH)

    own_copies = [
        pltpu.make_async_copy(stiff_hbm, own_s, own_sem.at[0]),
        pltpu.make_async_copy(mass_hbm, own_m, own_sem.at[1]),
        pltpu.make_async_copy(factor_hbm, own_w, own_sem.at[2]),
        pltpu.make_async_copy(shifts_hbm, shifts, own_sem.at[3]),
    ]
    for copy in own_copies:
        copy.start()

    row = lax.broadcasted_iota(jnp.int32, (512, 512), 0)
    col = lax.broadcasted_iota(jnp.int32, (512, 512), 1)
    perm[...] = jnp.where(row == CHUNK * (col % HALF) + col // HALF, 1.0, 0.0).astype(BF16)

    lane = lax.broadcasted_iota(jnp.int32, (8, LANES), 1)
    left = lane < HALF
    sub = lax.broadcasted_iota(jnp.int32, (8, LANES), 0)
    halves8 = jnp.where((sub % 2 == 0) == left, 1.0, 0.0).astype(BF16)
    sub16 = lax.broadcasted_iota(jnp.int32, (16, LANES), 0)
    lane16 = lax.broadcasted_iota(jnp.int32, (16, LANES), 1)
    halves16 = jnp.where(sub16 == lane16 // HALF, 1.0, 0.0).astype(BF16)
    lane1 = lax.broadcasted_iota(jnp.int32, (1, LANES), 1)
    left1 = lane1 < HALF
    first = k == 0
    last = k == chips - 1
    own = 2 + c

    for copy in own_copies:
        copy.wait()
    for e in range(18):
        lhs[4 * e:4 * e + 4, :] = own_s[e] if e < 9 else own_m[e - 9]
    moved = permuted(lhs[0:72, :], perm[...])
    for part in range(2):
        send_c[part] = moved[36 * part:36 * part + 36]
    moved = permuted(own_w[...].reshape(128, 512), perm[...])
    for core in range(2):
        for r in range(4):
            at = 32 * r + 16 * core
            for q in range(4):
                one = moved[at:at + 8, q * LANES:(q + 1) * LANES]
                two = moved[at + 8:at + 16, q * LANES:(q + 1) * LANES]
                send_w[core, r, 2 * q] = jnp.where(left, one, lane_roll(two, HALF))
                send_w[core, r, 2 * q + 1] = jnp.where(left, lane_roll(one, HALF), two)
    raw_c[own] = send_c[...]
    pb[0, pl.ds(4 * own, 4)] = send_w[c]

    pl.semaphore_wait(barrier, chips - 1 + 3)

    def field_copy(chip, core, block, sem):
        return pltpu.make_async_remote_copy(
            src_ref=send_w.at[core], dst_ref=pb.at[0, pl.ds(4 * block, 4)],
            send_sem=sem, recv_sem=in_recv.at[block, 2], device_id=device(chip, core), device_id_type=MESH)

    def stencil_copy(chip, core, block, part, sem):
        return pltpu.make_async_remote_copy(
            src_ref=send_c.at[part], dst_ref=raw_c.at[block, part],
            send_sem=sem, recv_sem=in_recv.at[block, part], device_id=device(chip, core), device_id_type=MESH)

    def hand_on(block, n):
        return pltpu.make_async_remote_copy(
            src_ref=raw_c.at[block, c], dst_ref=raw_c.at[block, c],
            send_sem=hand_send.at[n], recv_sem=in_recv.at[block, c], device_id=device(k, 1 - c), device_id_type=MESH)

    near_chip = lax.rem(k + 2 * c - 1 + chips, chips)
    far_chip = lax.rem(k + 1 - 2 * c + chips, chips)
    near_copies = [stencil_copy(near_chip, core, 4 - 3 * c, core, in_send.at[core, 0]) for core in range(2)]
    near_copies += [stencil_copy(k, 1 - c, own, part, in_send.at[2, part]) for part in range(2)]
    near_copies += [field_copy(near_chip, core, 4 - 3 * c, in_send.at[core, 1]) for core in range(2)]
    near_copies += [field_copy(k, 1 - c, own, in_send.at[2, 2])]
    far_copies = [stencil_copy(far_chip, core, 5 * c, core, far_send.at[core, 0]) for core in range(2)]
    far_copies += [field_copy(far_chip, core, 5 * c, far_send.at[core, 1]) for core in range(2)]
    for copy in near_copies:
        copy.start()

    def wait_part(block, part):
        half = raw_c.at[block, part]
        pltpu.make_async_copy(half, half, in_recv.at[block, part]).wait()

    def wait_field(block):
        rows = pb.at[0, pl.ds(4 * block, 4)]
        pltpu.make_async_copy(rows, rows, in_recv.at[block, 2]).wait()

    def wait_stencils(blocks):
        for block in blocks:
            wait_part(block, c)
            hand_on(block, block).start()
        for block in blocks:
            wait_part(block, 1 - c)

    def absent(block):
        if block < 2:
            return first
        if block > 3:
            return last
        return None

    def prepare(blocks, base):
        count = 4 * len(blocks)
        for e in range(18):
            for n, block in enumerate(blocks):
                value = raw_c[block, e // 9, 4 * (e % 9):4 * (e % 9) + 4, :]
                gone = absent(block)
                if gone is not None:
                    value = jnp.where(gone, 1.0 if e == 4 else 0.0, value)
                lhs[e * count + 4 * n:e * count + 4 * n + 4, :] = value
        for e in range(18):
            for q in range(4):
                value = lhs[e * count:(e + 1) * count, q * LANES:(q + 1) * LANES]
                other = lane_roll(value, HALF)
                both = [jnp.where(left1, value, other), jnp.where(left1, other, value)]
                if q == 0 and e % 3 == 0:
                    both[0] = jnp.where(lane1 % HALF == 0, 0.0, both[0])
                if q == 3 and e % 3 == 2:
                    both[1] = jnp.where(lane1 % HALF == HALF - 1, 0.0, both[1])
                for n in range(2):
                    ce[e * CHUNK + 2 * q + n, base:base + count, :] = both[n]

    def clear(block):
        @pl.when(absent(block))
        def _():
            pb[0, 4 * block:4 * block + 4] = jnp.zeros((4, CHUNK, 8, LANES), F32)

    def factor_rows(t, lo, hi):
        s = shifts[t]
        par = lax.rem(t, 2)

        def entry(e, m):
            return ce[e * CHUNK + m, lo:hi, :] + s * ce[(9 + e) * CHUNK + m, lo:hi, :]
        parts = line_factors(*[[entry(e, m) for m in range(CHUNK)] for e in (3, 4, 5)])
        for name, value in parts.items():
            fc[par, SLOT[name], lo:hi, :] = value
        for n, e in enumerate(OFF):
            for m in range(CHUNK):
                fc[par, len(NAMES) + n * CHUNK + m, lo:hi, :] = entry(e, m)

    def slot_of(r):
        return jnp.where(r < 4, r + 16, jnp.where(r < 20, r - 4, r))

    def line_group(par, it, rows):
        slots = [slot_of(r) for r in rows]

        def co(name, n):
            return fc[par, SLOT[name], pl.ds(slots[n], 1), :]

        g, d, ahead_g = [], [], []
        for n, r in enumerate(rows):
            v = [pb[it, r, m] for m in range(CHUNK)]
            for m in range(1, CHUNK - 1):
                v[m] = v[m] - co("w%d" % m, n) * v[m - 1]
            x = [v[m] * co("i%d" % m, n) for m in range(CHUNK - 1)]
            for m in reversed(range(CHUNK - 2)):
                x[m] = x[m] - co("u%d" % m, n) * x[m + 1]
            ahead_g.append(lane_roll(x[0], -1))
            d.append(v[-1] - co("a7", n) * x[-1] - co("c7", n) * ahead_g[-1])
            g.append(x)
        for level in range(3):
            step = 1 << (2 * level)
            new = []
            for n, v in enumerate(d):
                total = v if level < 2 else v * co("inv", n)
                for reach in (1, 2, 3):
                    total = total + (co("p%dd%d" % (level, reach), n) * lane_roll(v, reach * step)
                                     + co("p%du%d" % (level, reach), n) * lane_roll(v, -reach * step))
                new.append(total)
            d = new
        for n, r in enumerate(rows):
            after = d[n]
            before = lane_roll(after, 1)
            zb[it, r, 0] = before
            zb[it, r, CHUNK] = after
            for m in range(CHUNK - 1):
                zb[it, r, m + 1] = g[n][m] - co("e%d" % m, n) * before - co("f%d" % m, n) * after
            zb[it, r, CHUNK + 1] = ahead_g[n] - co("en", n) * after - co("fn", n) * lane_roll(after, -1)

    def off_row(par, it, r):
        slot = slot_of(r)
        for m in range(CHUNK):
            total = None
            for n, e in enumerate(OFF):
                source = zb[it, r + (-1 if e < 3 else 1), m + e % 3]
                term = fc[par, len(NAMES) + n * CHUNK + m, pl.ds(slot, 1), :] * source
                total = term if total is None else total + term
            pb[it + 1, r, m] = total

    def mass_row(it, n):
        for m in range(CHUNK):
            total = None
            for e in range(9):
                term = ce[(9 + e) * CHUNK + m, pl.ds(n + 4, 1), :] * zb[it, n + 7 + e // 3, m + e % 3]
                total = term if total is None else total + term
            mz[it, n, m] = total

    def send_halo(do):
        for n, (chip, at) in enumerate(((down, 8), (up, 12))):
            copy = pltpu.make_async_remote_copy(
                src_ref=pb.at[0, pl.ds(at, 4)], dst_ref=hx.at[n], send_sem=hx_send.at[n], recv_sem=hx_recv.at[n],
                device_id=device(chip, c), device_id_type=MESH)
            do(copy)

    def ar_copy(t, chip):
        return pltpu.make_async_remote_copy(
            src_ref=msg.at[t], dst_ref=arb.at[t, k], send_sem=ar_send.at[t], recv_sem=ar_recv.at[t],
            device_id=device(chip, c), device_id_type=MESH)

    def out_copies(n, dst):
        return (
            pltpu.make_async_copy(os_.at[n, pl.ds(4 * c, 4)], dst, out_local.at[n]),
            pltpu.make_async_remote_copy(
                src_ref=os_.at[n, pl.ds(4 - 4 * c, 4)], dst_ref=dst, send_sem=out_send.at[n], recv_sem=out_recv.at[n],
                device_id=device(k, 1 - c), device_id_type=MESH),
        )

    half_cols = pl.ds(pl.multiple_of(16 * c, 16), 16)

    def out_ref(n):
        return low_hbm.at[n, :, half_cols, :]

    def native(source):
        whole = left[None]
        tiles = [[], []]
        for q in range(4):
            even, odd = source[:, 2 * q], source[:, 2 * q + 1]
            tiles[0].append(jnp.where(whole, even, lane_roll(odd, HALF)).reshape(64, LANES))
            tiles[1].append(jnp.where(whole, lane_roll(even, HALF), odd).reshape(64, LANES))
        flat = jnp.concatenate([jnp.concatenate(t, axis=1) for t in tiles], axis=0)
        return permuted(flat, perm[...], 1).reshape(2, 8, 8, 512)

    def emit(n, source, dst):
        halves = native(source)
        for h in range(2):
            os_[n, :, 8 * h:8 * h + 8, :] = halves[h]
        for copy in out_copies(n, dst):
            copy.start()

    def emit_low(n):
        scale = jnp.sqrt(jnp.full((1, 1, 8, LANES), 2.0 * shifts[n], F32))
        emit(n, scale * ub[8:16, 1:CHUNK + 1], out_ref(n))

    for block in (2, 3):
        @pl.when(block == 3 - c)
        def _():
            for part in range(2):
                wait_part(block, part)
    wait_stencils((1, 4))
    prepare((1, 2, 3, 4), 0)
    factor_rows(0, 0, 16)
    for copy in near_copies:
        copy.wait_send()
    for copy in far_copies:
        copy.start()
    for block in (2, 3):
        @pl.when(block == 3 - c)
        def _():
            wait_field(block)
    for block in (1, 4):
        wait_field(block)
        clear(block)

    def adi(t, carry):
        s = shifts[t]
        par = lax.rem(t, 2)

        sums = {pair: jnp.zeros((8, LANES), F32) for pair in PAIRS}

        def dots(latest):
            for r in range(8, 16):
                for m in range(CHUNK):
                    newest = pb[latest, r, m]
                    for i in range(latest + 1):
                        sums[(i, latest)] = sums[(i, latest)] + newest * (newest if i == latest else pb[i, r, m])

        for it in range(ITERS):
            line_group(par, it, list(range(4 + it, 20 - it)))
            dots(it)

            def rows(n, carry):
                off_row(par, it, 5 + it + 2 * n)
                off_row(par, it, 6 + it + 2 * n)
                return carry
            lax.fori_loop(0, 7 - it, rows, 0)
        dots(ITERS)
        stacked = jnp.concatenate([sums[pair] for pair in PAIRS] + [jnp.zeros((8, LANES), F32)], axis=0)
        packed = lax.dot_general(halves16, jnp.concatenate(split3(stacked), axis=0), (((1,), (1,)), ((), ())), preferred_element_type=F32)
        packed = packed[0:2, 0:LANES] + packed[0:2, LANES:2 * LANES] + packed[0:2, 2 * LANES:]
        msg[t] = packed
        arb[t, k] = packed

        for chip in others:
            ar_copy(t, chip).start()

        @pl.when(t < 2)
        def _():
            factor_rows(t + 1, 0, 16)

        @pl.when(t > 0)
        def _():
            emit_low(t - 1)

        def images(n, carry):
            it = n // 4
            r = 2 * (n % 4)
            mass_row(it, r)
            mass_row(it, r + 1)
            return carry
        lax.fori_loop(0, 4 * ITERS, images, 0)

        @pl.when(t == 0)
        def _():
            wait_stencils((0, 5))
            prepare((0, 5), 16)
            factor_rows(0, 16, 24)
            factor_rows(1, 16, 24)
            for block in (0, 5):
                wait_field(block)
                clear(block)

        @pl.when(t == 1)
        def _():
            send_halo(lambda copy: copy.wait())
            for n, at in enumerate((0, 20)):
                gone = first if n == 0 else last
                for r in range(4):
                    pb[0, at + r] = jnp.where(gone, 0.0, hx[n, r])

        @pl.when(t < 2)
        def _():
            def outer(it, carry):
                line_group(par, it, [it + n for n in range(4)] + [20 - it + n for n in range(4)])

                @pl.when(it < ITERS - 1)
                def _():
                    def rows(n, carry):
                        off_row(par, it, it + 1 + n)
                        off_row(par, it, 19 - it + n)
                        return carry
                    lax.fori_loop(0, 4, rows, 0)
                return carry
            lax.fori_loop(0, ITERS, outer, 0)

        pltpu.make_async_copy(arb.at[t, pl.ds(0, chips - 1)], arb.at[t, pl.ds(0, chips - 1)], ar_recv.at[t]).wait()
        total = jnp.sum(arb[t], axis=0)
        total = jnp.concatenate([total] * 3 + [jnp.zeros((2, LANES), F32)], axis=0)
        one, two, three = [part.astype(F32) for part in split3(total)]
        total = jnp.where(sub < 2, one, jnp.where(sub < 4, two, three)).astype(BF16)
        spread_out = lax.dot_general(total, halves8, (((0,), (0,)), ((), ())), preferred_element_type=F32)
        gram = {pair: spread_out[8 * n:8 * n + 8] for n, pair in enumerate(PAIRS)}
        y = solve_weights(gram)

        def combine(r, carry):
            for m in range(CHUNK + 2):
                total = y[0] * zb[0, r, m]
                for it in range(1, ITERS):
                    total = total + y[it] * zb[it, r, m]
                ub[r, m] = total
            return carry

        twice = 2.0 * s

        def update(r, carry):
            slot = slot_of(r)
            for m in range(CHUNK):
                total = None
                for e in range(9):
                    term = ce[(9 + e) * CHUNK + m, pl.ds(slot, 1), :] * ub[r + e // 3 - 1, m + e % 3]
                    total = term if total is None else total + term
                pb[0, r, m] = pb[0, r, m] - twice * total
            return carry
        scaled = [twice * value for value in y]

        def update_own(n, carry):
            for m in range(CHUNK):
                total = scaled[0] * mz[0, n, m]
                for it in range(1, ITERS):
                    total = total + scaled[it] * mz[it, n, m]
                pb[0, 8 + n, m] = pb[0, 8 + n, m] - total
            return carry
        lax.fori_loop(0, 8, update_own, 0, unroll=2)

        @pl.when(t == 0)
        def _():
            send_halo(lambda copy: copy.start())

        lax.fori_loop(8, 16, combine, 0, unroll=2)

        @pl.when(t < 2)
        def _():
            lax.fori_loop(3, 8, combine, 0)
            lax.fori_loop(16, 21, combine, 0)
            lax.fori_loop(4, 8, update, 0, unroll=2)
            lax.fori_loop(16, 20, update, 0, unroll=2)
        return carry

    lax.fori_loop(0, STEPS, adi, 0)

    res_at = res_hbm.at[:, half_cols, :]
    emit_low(STEPS - 1)
    emit(STEPS, pb[0, 8:16], res_at)

    for copy in far_copies:
        copy.wait_send()
    for block in (0, 1, 4, 5):
        hand_on(block, block).wait_send()

    def drain(t, carry):
        pltpu.make_async_copy(arb.at[t, pl.ds(0, chips - 1)], arb.at[t, pl.ds(0, chips - 1)], ar_send.at[t]).wait()
        for copy in out_copies(t, out_ref(t)):
            copy.wait()
        return carry
    lax.fori_loop(0, STEPS, drain, 0)
    for copy in out_copies(STEPS, res_at):
        copy.wait()


def solution(mesh):
    chips = mesh.shape["rows"] // 2

    def shards(stiffness, mass, shifts, factor):
        field = (24, CHUNK, 8, LANES)
        framed = (24, CHUNK + 2, 8, LANES)
        dma = pltpu.SemaphoreType.DMA
        return pl.pallas_call(
            functools.partial(kernel, chips),
            out_shape=(jax.ShapeDtypeStruct((STEPS, 4, 32, 512), F32), jax.ShapeDtypeStruct((4, 32, 512), F32)),
            in_specs=[pl.BlockSpec(memory_space=pl.ANY)] * 4,
            out_specs=(pl.BlockSpec(memory_space=pl.ANY), pl.BlockSpec(memory_space=pl.ANY)),
            scratch_shapes=[
                pltpu.VMEM((512, 512), BF16),
                pltpu.VMEM((9, 4, 512), F32),
                pltpu.VMEM((9, 4, 512), F32),
                pltpu.VMEM((4, 32, 512), F32),
                pltpu.VMEM((18 * 16, 512), F32),
                pltpu.VMEM((2, 36, 512), F32),
                pltpu.VMEM((2, 4, CHUNK, 8, LANES), F32),
                pltpu.VMEM((6, 2, 36, 512), F32),
                pltpu.VMEM((18 * CHUNK, 24, LANES), F32),
                pltpu.VMEM((2, COUNT, 24, LANES), F32),
                pltpu.VMEM((ITERS + 1,) + field, F32),
                pltpu.VMEM((ITERS,) + framed, F32),
                pltpu.VMEM(framed, F32),
                pltpu.VMEM((ITERS, 8, CHUNK, 8, LANES), F32),
                pltpu.VMEM((STEPS + 1, 8, 16, 512), F32),
                pltpu.VMEM((STEPS, chips, 2, LANES), F32),
                pltpu.VMEM((2, 4, CHUNK, 8, LANES), F32),
                pltpu.VMEM((STEPS, 2, LANES), F32),
                pltpu.SMEM((STEPS,), F32),
                dma((4,)),
                dma((6,)),
                dma((3, 3)),
                dma((6, 3)),
                dma((2, 2)),
                dma((STEPS,)),
                dma((STEPS,)),
                dma((2,)),
                dma((2,)),
                dma((STEPS + 1,)),
                dma((STEPS + 1,)),
                dma((STEPS + 1,)),
            ],
            compiler_params=pltpu.CompilerParams(
                collective_id=0, has_side_effects=True, vmem_limit_bytes=60 << 20),
        )(shifts, stiffness, mass, factor)

    return jax.shard_map(
        shards,
        mesh=mesh,
        in_specs=(P(None, "rows", None), P(None, "rows", None), P(), P("rows", None, None)),
        out_specs=(P(None, "rows", None, None), P("rows", None, None)),
        check_vma=False,
    )
```

```python
import functools

import jax
import jax.numpy as jnp
from jax import lax
from jax.experimental import pallas as pl
from jax.experimental.pallas import tpu as pltpu
from jax.sharding import PartitionSpec as P

STEPS = 3
ITERS = 4
MESH = pl.DeviceIdType.MESH
PAIRS = [(i, j) for i in range(ITERS + 1) for j in range(i, ITERS + 1)]
LANES = 128
CHUNK = 8
HALF = 64
F32 = jnp.float32
BF16 = jnp.bfloat16

NAMES = ["w%d" % n for n in range(1, 7)] + ["i%d" % n for n in range(7)] + ["u%d" % n for n in range(6)]
NAMES += ["e%d" % n for n in range(7)] + ["f%d" % n for n in range(7)] + ["a7", "c7", "inv", "en", "fn"]
NAMES += ["p%d%s%d" % (level, way, reach) for level in range(3) for way in "du" for reach in (1, 2, 3)]
SLOT = {name: n for n, name in enumerate(NAMES)}
OFF = (0, 1, 2, 6, 7, 8)
COUNT = len(NAMES) + len(OFF) * CHUNK


def lane_roll(x, shift):
    return pltpu.roll(x, shift % LANES, axis=x.ndim - 1)


def split3(x):
    a = x.astype(BF16)
    rest = x - a.astype(F32)
    b = rest.astype(BF16)
    c = (rest - b.astype(F32)).astype(BF16)
    return a, b, c


def permuted(x, perm, dim=0):
    rows = x.shape[0]
    moved = lax.dot_general(jnp.concatenate(split3(x), axis=0), perm, (((1,), (dim,)), ((), ())), preferred_element_type=F32)
    return moved[:rows] + moved[rows:2 * rows] + moved[2 * rows:]


def line_factors(a, b, c):
    out = {}
    last = CHUNK - 1
    i, u, w = [], [], [None]
    for m in range(last):
        pivot = b[m]
        if m:
            w.append(a[m] * i[m - 1])
            pivot = pivot - w[m] * c[m - 1]
        i.append(1.0 / pivot)
        u.append(c[m] * i[m])
    t = [a[0]]
    for m in range(1, last):
        t.append(-w[m] * t[m - 1])
    e, f = [None] * last, [None] * last
    e[last - 1] = t[last - 1] * i[last - 1]
    f[last - 1] = u[last - 1]
    for m in reversed(range(last - 1)):
        e[m] = t[m] * i[m] - u[m] * e[m + 1]
        f[m] = -u[m] * f[m + 1]
    for m in range(last):
        out["i%d" % m], out["e%d" % m], out["f%d" % m] = i[m], e[m], f[m]
        if m:
            out["w%d" % m] = w[m]
        if m < last - 1:
            out["u%d" % m] = u[m]
    out["a7"], out["c7"] = a[last], c[last]
    out["en"], out["fn"] = lane_roll(e[0], -1), lane_roll(f[0], -1)
    low = -a[last] * e[last - 1]
    mid = b[last] - a[last] * f[last - 1] - c[last] * out["en"]
    high = -c[last] * out["fn"]
    for level in range(3):
        k = 1 << (2 * level)
        pairs = []
        for reach in (k, 2 * k):
            inv = 1.0 / mid
            al = -low * lane_roll(inv, reach)
            ga = -high * lane_roll(inv, -reach)
            mid = mid + al * lane_roll(high, reach) + ga * lane_roll(low, -reach)
            low, high = al * lane_roll(low, reach), ga * lane_roll(high, -reach)
            pairs.append((al, ga))
        (al1, ga1), (al2, ga2) = pairs
        merged = {
            "d1": al1 + al2 * lane_roll(ga1, 2 * k), "d2": al2, "d3": al2 * lane_roll(al1, 2 * k),
            "u1": ga1 + ga2 * lane_roll(al1, -2 * k), "u2": ga2, "u3": ga2 * lane_roll(ga1, -2 * k),
        }
        for key, value in merged.items():
            out["p%d%s" % (level, key)] = value
    inv = 1.0 / mid
    out["inv"] = inv
    for key in ("d1", "d2", "d3", "u1", "u2", "u3"):
        out["p2" + key] = out["p2" + key] * inv
    return out


def least_squares(columns, initial):
    count = len(columns)
    cosines, sines = [], []
    rhs = [initial] + [None] * count
    upper = []
    for position in range(count):
        column = list(columns[position])
        for earlier in range(position):
            first = cosines[earlier] * column[earlier] + sines[earlier] * column[earlier + 1]
            second = -sines[earlier] * column[earlier] + cosines[earlier] * column[earlier + 1]
            column[earlier], column[earlier + 1] = first, second
        radius = jnp.sqrt(column[position] * column[position] + column[position + 1] * column[position + 1])
        inverse = 1.0 / radius
        cosine = column[position] * inverse
        sine = column[position + 1] * inverse
        cosines.append(cosine)
        sines.append(sine)
        rhs[position + 1] = -sine * rhs[position]
        rhs[position] = cosine * rhs[position]
        upper.append(column[:position] + [inverse])
    y = [None] * count
    for position in reversed(range(count)):
        accum = rhs[position]
        for onward in range(position + 1, count):
            accum = accum - upper[onward][position] * y[onward]
        y[position] = accum * upper[position][position]
    return y


def solve_weights(gram):
    n = ITERS + 1
    r = {}
    for i in range(n):
        pivot = gram[(i, i)]
        for m in range(i):
            pivot = pivot - r[(m, i)] * r[(m, i)]
        pivot = jnp.maximum(pivot, gram[(i, i)] * 1e-9)
        root = jnp.sqrt(pivot)
        r[(i, i)] = root
        inverse = 1.0 / root
        for j in range(i + 1, n):
            value = gram[(i, j)]
            for m in range(i):
                value = value - r[(m, i)] * r[(m, j)]
            r[(i, j)] = value * inverse
    columns = []
    for k in range(ITERS):
        columns.append([r[(i, k)] + r[(i, k + 1)] for i in range(k + 1)] + [r[(k + 1, k + 1)]])
    return least_squares(columns, r[(0, 0)])


def kernel(chips, shifts_hbm, stiff_hbm, mass_hbm, factor_hbm, low_hbm, res_hbm,
           perm, own_s, own_m, own_w, lhs, send_c, send_w, raw_c, ce, fc, pb, zb, ub, mz, zn, os_, arb, hx, msg, shifts,
           own_sem, in_send, in_recv, far_send, ar_send, ar_recv, hx_send, hx_recv, out_send, out_recv, out_local):
    me = lax.axis_index("rows")
    k = me // 2
    c = me % 2
    up = lax.rem(k + chips - 1, chips)
    down = lax.rem(k + 1, chips)

    def device(chip, core):
        return (chip * 2 + core,)

    barrier = pltpu.get_barrier_semaphore()

    if chips == 64:
        ahead = [[lax.rem(lax.div(k, stride) + n, 4) * stride for n in range(4)] for stride in (16, 4, 1)]
        spans = sorted(
            ((a, b, d) for a in range(4) for b in range(4) for d in range(4) if (a, b, d) != (0, 0, 0)),
            key=lambda offset: -sum(min(n, 4 - n) for n in offset))
        others = [ahead[0][a] + ahead[1][b] + ahead[2][d] for a, b, d in spans]
    else:
        others = [lax.rem(k + n, chips) for n in range(1, chips)]

    for chip in (up, down, k):
        pl.semaphore_signal(barrier, inc=1, device_id=device(chip, 1 - c), device_id_type=MESH)
    for chip in others:
        pl.semaphore_signal(barrier, inc=1, device_id=device(chip, c), device_id_type=MESH)

    own_copies = [
        pltpu.make_async_copy(stiff_hbm, own_s, own_sem.at[0]),
        pltpu.make_async_copy(mass_hbm, own_m, own_sem.at[1]),
        pltpu.make_async_copy(factor_hbm, own_w, own_sem.at[2]),
        pltpu.make_async_copy(shifts_hbm, shifts, own_sem.at[3]),
    ]
    for copy in own_copies:
        copy.start()

    row = lax.broadcasted_iota(jnp.int32, (512, 512), 0)
    col = lax.broadcasted_iota(jnp.int32, (512, 512), 1)
    perm[...] = jnp.where(row == CHUNK * (col % HALF) + col // HALF, 1.0, 0.0).astype(BF16)

    lane = lax.broadcasted_iota(jnp.int32, (8, LANES), 1)
    left = lane < HALF
    sub = lax.broadcasted_iota(jnp.int32, (8, LANES), 0)
    halves8 = jnp.where((sub % 2 == 0) == left, 1.0, 0.0).astype(BF16)
    sub16 = lax.broadcasted_iota(jnp.int32, (16, LANES), 0)
    lane16 = lax.broadcasted_iota(jnp.int32, (16, LANES), 1)
    halves16 = jnp.where(sub16 == lane16 // HALF, 1.0, 0.0).astype(BF16)
    lane1 = lax.broadcasted_iota(jnp.int32, (1, LANES), 1)
    left1 = lane1 < HALF
    first = k == 0
    last = k == chips - 1
    own = 2 + c

    for copy in own_copies:
        copy.wait()
    for e in range(18):
        lhs[4 * e:4 * e + 4, :] = own_s[e] if e < 9 else own_m[e - 9]
    send_c[...] = permuted(lhs[0:72, :], perm[...])
    moved = permuted(own_w[...].reshape(128, 512), perm[...])
    for core in range(2):
        for r in range(4):
            at = 32 * r + 16 * core
            for q in range(4):
                one = moved[at:at + 8, q * LANES:(q + 1) * LANES]
                two = moved[at + 8:at + 16, q * LANES:(q + 1) * LANES]
                send_w[core, r, 2 * q] = jnp.where(left, one, lane_roll(two, HALF))
                send_w[core, r, 2 * q + 1] = jnp.where(left, lane_roll(one, HALF), two)
    raw_c[own] = send_c[...]
    pb[0, pl.ds(4 * own, 4)] = send_w[c]

    pl.semaphore_wait(barrier, chips - 1 + 3)

    def block_copies(chip, core, block, sems):
        return [
            pltpu.make_async_remote_copy(
                src_ref=send_c, dst_ref=raw_c.at[block],
                send_sem=sems.at[0], recv_sem=in_recv.at[block, 0], device_id=device(chip, core), device_id_type=MESH),
            pltpu.make_async_remote_copy(
                src_ref=send_w.at[core], dst_ref=pb.at[0, pl.ds(4 * block, 4)],
                send_sem=sems.at[1], recv_sem=in_recv.at[block, 1], device_id=device(chip, core), device_id_type=MESH),
        ]

    near_chip = lax.rem(k + 2 * c - 1 + chips, chips)
    far_chip = lax.rem(k + 1 - 2 * c + chips, chips)
    near_copies, far_copies = [], []
    for core in range(2):
        near_copies.append(block_copies(near_chip, core, 4 - 3 * c, in_send.at[core]))
        far_copies += block_copies(far_chip, core, 5 * c, far_send.at[core])
    near_copies.append(block_copies(k, 1 - c, own, in_send.at[2]))
    near_copies = [pair[0] for pair in near_copies] + [pair[1] for pair in near_copies]
    for copy in near_copies:
        copy.start()

    def wait_stencil(block):
        pltpu.make_async_copy(raw_c.at[block], raw_c.at[block], in_recv.at[block, 0]).wait()

    def wait_field(block):
        rows = pb.at[0, pl.ds(4 * block, 4)]
        pltpu.make_async_copy(rows, rows, in_recv.at[block, 1]).wait()

    def absent(block):
        if block < 2:
            return first
        if block > 3:
            return last
        return None

    def prepare(blocks, base):
        count = 4 * len(blocks)
        for e in range(18):
            for n, block in enumerate(blocks):
                value = raw_c[block, 4 * e:4 * e + 4, :]
                gone = absent(block)
                if gone is not None:
                    value = jnp.where(gone, 1.0 if e == 4 else 0.0, value)
                lhs[e * count + 4 * n:e * count + 4 * n + 4, :] = value
        for e in range(18):
            for q in range(4):
                value = lhs[e * count:(e + 1) * count, q * LANES:(q + 1) * LANES]
                other = lane_roll(value, HALF)
                both = [jnp.where(left1, value, other), jnp.where(left1, other, value)]
                if q == 0 and e % 3 == 0:
                    both[0] = jnp.where(lane1 % HALF == 0, 0.0, both[0])
                if q == 3 and e % 3 == 2:
                    both[1] = jnp.where(lane1 % HALF == HALF - 1, 0.0, both[1])
                for n in range(2):
                    ce[e * CHUNK + 2 * q + n, base:base + count, :] = both[n]

    def clear(block):
        @pl.when(absent(block))
        def _():
            pb[0, 4 * block:4 * block + 4] = jnp.zeros((4, CHUNK, 8, LANES), F32)

    def factor_rows(t, lo, hi):
        s = shifts[t]
        par = lax.rem(t, 2)

        def entry(e, m):
            return ce[e * CHUNK + m, lo:hi, :] + s * ce[(9 + e) * CHUNK + m, lo:hi, :]
        parts = line_factors(*[[entry(e, m) for m in range(CHUNK)] for e in (3, 4, 5)])
        for name, value in parts.items():
            fc[par, SLOT[name], lo:hi, :] = value
        for n, e in enumerate(OFF):
            for m in range(CHUNK):
                fc[par, len(NAMES) + n * CHUNK + m, lo:hi, :] = entry(e, m)

    def slot_of(r):
        if isinstance(r, int):
            return r + 16 if r < 4 else (r - 4 if r < 20 else r)
        return jnp.where(r < 4, r + 16, jnp.where(r < 20, r - 4, r))

    def line_group(par, it, rows):
        slots = [slot_of(r) for r in rows]

        def co(name, n):
            return fc[par, SLOT[name], pl.ds(slots[n], 1), :]

        g, d, ahead_g = [], [], []
        for n, r in enumerate(rows):
            v = [pb[it, r, m] for m in range(CHUNK)]
            for m in range(1, CHUNK - 1):
                v[m] = v[m] - co("w%d" % m, n) * v[m - 1]
            x = [v[m] * co("i%d" % m, n) for m in range(CHUNK - 1)]
            for m in reversed(range(CHUNK - 2)):
                x[m] = x[m] - co("u%d" % m, n) * x[m + 1]
            ahead_g.append(lane_roll(x[0], -1))
            d.append(v[-1] - co("a7", n) * x[-1] - co("c7", n) * ahead_g[-1])
            g.append(x)
        for level in range(3):
            step = 1 << (2 * level)
            new = []
            for n, v in enumerate(d):
                total = v if level < 2 else v * co("inv", n)
                for reach in (1, 2, 3):
                    total = total + (co("p%dd%d" % (level, reach), n) * lane_roll(v, reach * step)
                                     + co("p%du%d" % (level, reach), n) * lane_roll(v, -reach * step))
                new.append(total)
            d = new
        for n, r in enumerate(rows):
            after = d[n]
            before = lane_roll(after, 1)
            zb[it, r, 0] = before
            zb[it, r, CHUNK] = after
            for m in range(CHUNK - 1):
                zb[it, r, m + 1] = g[n][m] - co("e%d" % m, n) * before - co("f%d" % m, n) * after
            zb[it, r, CHUNK + 1] = ahead_g[n] - co("en", n) * after - co("fn", n) * lane_roll(after, -1)

    def off_row(par, it, r):
        slot = slot_of(r)
        for m in range(CHUNK):
            total = None
            for n, e in enumerate(OFF):
                source = zb[it, r + (-1 if e < 3 else 1), m + e % 3]
                term = fc[par, len(NAMES) + n * CHUNK + m, pl.ds(slot, 1), :] * source
                total = term if total is None else total + term
            pb[it + 1, r, m] = total

    def mass_row(it, n):
        for m in range(CHUNK):
            total = None
            for e in range(9):
                term = ce[(9 + e) * CHUNK + m, pl.ds(n + 4, 1), :] * zb[it, n + 7 + e // 3, m + e % 3]
                total = term if total is None else total + term
            mz[it, n, m] = total

    def send_halo(do):
        for n, (chip, at) in enumerate(((down, 8), (up, 12))):
            copy = pltpu.make_async_remote_copy(
                src_ref=pb.at[0, pl.ds(at, 4)], dst_ref=hx.at[n], send_sem=hx_send.at[n], recv_sem=hx_recv.at[n],
                device_id=device(chip, c), device_id_type=MESH)
            do(copy)

    def ar_copy(t, chip):
        return pltpu.make_async_remote_copy(
            src_ref=msg.at[t], dst_ref=arb.at[t, k], send_sem=ar_send.at[t], recv_sem=ar_recv.at[t],
            device_id=device(chip, c), device_id_type=MESH)

    def out_copies(n, dst):
        return (
            pltpu.make_async_copy(os_.at[n, pl.ds(4 * c, 4)], dst, out_local.at[n]),
            pltpu.make_async_remote_copy(
                src_ref=os_.at[n, pl.ds(4 - 4 * c, 4)], dst_ref=dst, send_sem=out_send.at[n], recv_sem=out_recv.at[n],
                device_id=device(k, 1 - c), device_id_type=MESH),
        )

    half_cols = pl.ds(pl.multiple_of(16 * c, 16), 16)

    def out_ref(n):
        return low_hbm.at[n, :, half_cols, :]

    def native(source):
        whole = left[None]
        tiles = [[], []]
        for q in range(4):
            even, odd = source[:, 2 * q], source[:, 2 * q + 1]
            tiles[0].append(jnp.where(whole, even, lane_roll(odd, HALF)).reshape(64, LANES))
            tiles[1].append(jnp.where(whole, lane_roll(even, HALF), odd).reshape(64, LANES))
        flat = jnp.concatenate([jnp.concatenate(t, axis=1) for t in tiles], axis=0)
        return permuted(flat, perm[...], 1).reshape(2, 8, 8, 512)

    def emit(n, source, dst):
        halves = native(source)
        for h in range(2):
            os_[n, :, 8 * h:8 * h + 8, :] = halves[h]
        for copy in out_copies(n, dst):
            copy.start()

    def emit_low(n):
        scale = jnp.sqrt(jnp.full((1, 1, 8, LANES), 2.0 * shifts[n], F32))
        emit(n, scale * ub[8:16, 1:CHUNK + 1], out_ref(n))

    for block in (2, 3):
        @pl.when(block == 3 - c)
        def _():
            wait_stencil(block)
    wait_stencil(1)
    wait_stencil(4)
    prepare((1, 2, 3, 4), 0)
    factor_rows(0, 0, 16)
    for copy in near_copies:
        copy.wait_send()
    for copy in far_copies:
        copy.start()
    for block in (2, 3):
        @pl.when(block == 3 - c)
        def _():
            wait_field(block)
    for block in (1, 4):
        wait_field(block)
        clear(block)

    def adi(t, carry):
        s = shifts[t]
        par = lax.rem(t, 2)

        sums = {pair: jnp.zeros((8, LANES), F32) for pair in PAIRS}

        def dots(latest):
            for r in range(8, 16):
                for m in range(CHUNK):
                    newest = pb[latest, r, m]
                    for i in range(latest + 1):
                        sums[(i, latest)] = sums[(i, latest)] + newest * (newest if i == latest else pb[i, r, m])

        for it in range(ITERS):
            line_group(par, it, list(range(4 + it, 20 - it)))
            dots(it)

            for r in range(5 + it, 19 - it):
                off_row(par, it, r)
        dots(ITERS)
        stacked = jnp.concatenate([sums[pair] for pair in PAIRS] + [jnp.zeros((8, LANES), F32)], axis=0)
        packed = lax.dot_general(halves16, jnp.concatenate(split3(stacked), axis=0), (((1,), (1,)), ((), ())), preferred_element_type=F32)
        packed = packed[0:2, 0:LANES] + packed[0:2, LANES:2 * LANES] + packed[0:2, 2 * LANES:]
        msg[t] = packed
        arb[t, k] = packed

        for chip in others:
            ar_copy(t, chip).start()

        @pl.when(t < 2)
        def _():
            factor_rows(t + 1, 0, 16)

        @pl.when(t > 0)
        def _():
            emit_low(t - 1)

        @pl.when(t == 0)
        def _():
            for block in (0, 5):
                wait_stencil(block)
            prepare((0, 5), 16)
            factor_rows(0, 16, 24)
            factor_rows(1, 16, 24)
            for block in (0, 5):
                wait_field(block)
                clear(block)

        @pl.when(t == 1)
        def _():
            send_halo(lambda copy: copy.wait())
            for n, at in enumerate((0, 20)):
                gone = first if n == 0 else last
                for r in range(4):
                    pb[0, at + r] = jnp.where(gone, 0.0, hx[n, r])

        @pl.when(t < 2)
        def _():
            def outer(it, carry):
                line_group(par, it, [it + n for n in range(4)] + [20 - it + n for n in range(4)])

                @pl.when(it < ITERS - 1)
                def _():
                    def rows(n, carry):
                        off_row(par, it, it + 1 + n)
                        off_row(par, it, 19 - it + n)
                        return carry
                    lax.fori_loop(0, 4, rows, 0)
                return carry
            lax.fori_loop(0, ITERS, outer, 0)

        @pl.when(t == STEPS - 1)
        def _():
            def images(n, carry):
                mass_row(n // 4, 2 * (n % 4))
                mass_row(n // 4, 2 * (n % 4) + 1)
                return carry
            lax.fori_loop(0, 4 * ITERS, images, 0)

            def reorder(it, carry):
                zn[it] = native(zb[it, 8:16, 1:CHUNK + 1])
                zn[ITERS + it] = native(mz[it])
                return carry
            lax.fori_loop(0, ITERS, reorder, 0)
            zn[2 * ITERS] = native(pb[0, 8:16])

        pltpu.make_async_copy(arb.at[t, pl.ds(0, chips - 1)], arb.at[t, pl.ds(0, chips - 1)], ar_recv.at[t]).wait()
        total = jnp.sum(arb[t], axis=0)
        total = jnp.concatenate([total] * 3 + [jnp.zeros((2, LANES), F32)], axis=0)
        one, two, three = [part.astype(F32) for part in split3(total)]
        total = jnp.where(sub < 2, one, jnp.where(sub < 4, two, three)).astype(BF16)
        spread_out = lax.dot_general(total, halves8, (((0,), (0,)), ((), ())), preferred_element_type=F32)
        gram = {pair: spread_out[8 * n:8 * n + 8] for n, pair in enumerate(PAIRS)}
        y = solve_weights(gram)

        def combine(r, carry):
            for m in range(CHUNK + 2):
                total = y[0] * zb[0, r, m]
                for it in range(1, ITERS):
                    total = total + y[it] * zb[it, r, m]
                ub[r, m] = total
            return carry

        twice = 2.0 * s

        def update(r, carry):
            slot = slot_of(r)
            for m in range(CHUNK):
                total = None
                for e in range(9):
                    term = ce[(9 + e) * CHUNK + m, pl.ds(slot, 1), :] * ub[r + e // 3 - 1, m + e % 3]
                    total = term if total is None else total + term
                pb[0, r, m] = pb[0, r, m] - twice * total
            return carry
        @pl.when(t < STEPS - 1)
        def _():
            for r in range(7, 17):
                combine(r, 0)
            for r in range(8, 16):
                update(r, 0)

        @pl.when(t == 0)
        def _():
            send_halo(lambda copy: copy.start())

        @pl.when(t < STEPS - 1)
        def _():
            for r in list(range(3, 7)) + list(range(17, 21)):
                combine(r, 0)
            for r in list(range(4, 8)) + list(range(16, 20)):
                update(r, 0)

        @pl.when(t == STEPS - 1)
        def _():
            both = []
            for value in y:
                other = lane_roll(value, HALF)
                both.append((jnp.where(left, value, other), jnp.where(left, other, value)))
            scale = jnp.sqrt(jnp.full((8, LANES), twice, F32))

            def weighted(base, factor, h, r, span):
                total = (factor * both[0][h]) * zn[base, h, r, :, span]
                for it in range(1, ITERS):
                    total = total + (factor * both[it][h]) * zn[base + it, h, r, :, span]
                return total

            def low_row(r, carry):
                for h in range(2):
                    for q in range(4):
                        span = slice(q * LANES, (q + 1) * LANES)
                        os_[STEPS - 1, r, 8 * h:8 * h + 8, span] = weighted(0, scale, h, r, span)
                return carry

            def res_row(r, carry):
                for h in range(2):
                    for q in range(4):
                        span = slice(q * LANES, (q + 1) * LANES)
                        os_[STEPS, r, 8 * h:8 * h + 8, span] = zn[2 * ITERS, h, r, :, span] - weighted(ITERS, twice, h, r, span)
                return carry
            lax.fori_loop(0, 8, low_row, 0, unroll=2)
            for copy in out_copies(STEPS - 1, out_ref(STEPS - 1)):
                copy.start()
            lax.fori_loop(0, 8, res_row, 0, unroll=2)
            for copy in out_copies(STEPS, res_at):
                copy.start()
        return carry

    res_at = res_hbm.at[:, half_cols, :]
    lax.fori_loop(0, STEPS, adi, 0)

    for copy in far_copies:
        copy.wait_send()

    def drain(t, carry):
        pltpu.make_async_copy(arb.at[t, pl.ds(0, chips - 1)], arb.at[t, pl.ds(0, chips - 1)], ar_send.at[t]).wait()
        for copy in out_copies(t, out_ref(t)):
            copy.wait()
        return carry
    lax.fori_loop(0, STEPS, drain, 0)
    for copy in out_copies(STEPS, res_at):
        copy.wait()


def solution(mesh):
    chips = mesh.shape["rows"] // 2

    def shards(stiffness, mass, shifts, factor):
        field = (24, CHUNK, 8, LANES)
        framed = (24, CHUNK + 2, 8, LANES)
        dma = pltpu.SemaphoreType.DMA
        return pl.pallas_call(
            functools.partial(kernel, chips),
            out_shape=(jax.ShapeDtypeStruct((STEPS, 4, 32, 512), F32), jax.ShapeDtypeStruct((4, 32, 512), F32)),
            in_specs=[pl.BlockSpec(memory_space=pl.ANY)] * 4,
            out_specs=(pl.BlockSpec(memory_space=pl.ANY), pl.BlockSpec(memory_space=pl.ANY)),
            scratch_shapes=[
                pltpu.VMEM((512, 512), BF16),
                pltpu.VMEM((9, 4, 512), F32),
                pltpu.VMEM((9, 4, 512), F32),
                pltpu.VMEM((4, 32, 512), F32),
                pltpu.VMEM((18 * 16, 512), F32),
                pltpu.VMEM((18 * 4, 512), F32),
                pltpu.VMEM((2, 4, CHUNK, 8, LANES), F32),
                pltpu.VMEM((6, 18 * 4, 512), F32),
                pltpu.VMEM((18 * CHUNK, 24, LANES), F32),
                pltpu.VMEM((2, COUNT, 24, LANES), F32),
                pltpu.VMEM((ITERS + 1,) + field, F32),
                pltpu.VMEM((ITERS,) + framed, F32),
                pltpu.VMEM(framed, F32),
                pltpu.VMEM((ITERS, 8, CHUNK, 8, LANES), F32),
                pltpu.VMEM((2 * ITERS + 1, 2, 8, 8, 512), F32),
                pltpu.VMEM((STEPS + 1, 8, 16, 512), F32),
                pltpu.VMEM((STEPS, chips, 2, LANES), F32),
                pltpu.VMEM((2, 4, CHUNK, 8, LANES), F32),
                pltpu.VMEM((STEPS, 2, LANES), F32),
                pltpu.SMEM((STEPS,), F32),
                dma((4,)),
                dma((3, 2)),
                dma((6, 2)),
                dma((2, 2)),
                dma((STEPS,)),
                dma((STEPS,)),
                dma((2,)),
                dma((2,)),
                dma((STEPS + 1,)),
                dma((STEPS + 1,)),
                dma((STEPS + 1,)),
            ],
            compiler_params=pltpu.CompilerParams(
                collective_id=0, has_side_effects=True, vmem_limit_bytes=60 << 20),
        )(shifts, stiffness, mass, factor)

    return jax.shard_map(
        shards,
        mesh=mesh,
        in_specs=(P(None, "rows", None), P(None, "rows", None), P(), P("rows", None, None)),
        out_specs=(P(None, "rows", None, None), P("rows", None, None)),
        check_vma=False,
    )
```

```python
import functools

import jax
import jax.numpy as jnp
from jax import lax
from jax.experimental import pallas as pl
from jax.experimental.pallas import tpu as pltpu
from jax.sharding import PartitionSpec as P

STEPS = 3
ITERS = 4
MESH = pl.DeviceIdType.MESH
PAIRS = [(i, j) for i in range(ITERS + 1) for j in range(i, ITERS + 1)]
LANES = 128
CHUNK = 8
HALF = 64
F32 = jnp.float32
BF16 = jnp.bfloat16

NAMES = ["w%d" % n for n in range(1, 7)] + ["i%d" % n for n in range(7)] + ["u%d" % n for n in range(6)]
NAMES += ["e%d" % n for n in range(7)] + ["f%d" % n for n in range(7)] + ["a7", "c7", "inv", "en", "fn"]
NAMES += ["p%d%s%d" % (level, way, reach) for level in range(3) for way in "du" for reach in (1, 2, 3)]
SLOT = {name: n for n, name in enumerate(NAMES)}
OFF = (0, 1, 2, 6, 7, 8)
COUNT = len(NAMES) + len(OFF) * CHUNK


def lane_roll(x, shift):
    return pltpu.roll(x, shift % LANES, axis=x.ndim - 1)


def split3(x):
    a = x.astype(BF16)
    rest = x - a.astype(F32)
    b = rest.astype(BF16)
    c = (rest - b.astype(F32)).astype(BF16)
    return a, b, c


def permuted(x, perm, dim=0):
    rows = x.shape[0]
    moved = lax.dot_general(jnp.concatenate(split3(x), axis=0), perm, (((1,), (dim,)), ((), ())), preferred_element_type=F32)
    return moved[:rows] + moved[rows:2 * rows] + moved[2 * rows:]


def line_factors(a, b, c):
    out = {}
    last = CHUNK - 1
    i, u, w = [], [], [None]
    for m in range(last):
        pivot = b[m]
        if m:
            w.append(a[m] * i[m - 1])
            pivot = pivot - w[m] * c[m - 1]
        i.append(1.0 / pivot)
        u.append(c[m] * i[m])
    t = [a[0]]
    for m in range(1, last):
        t.append(-w[m] * t[m - 1])
    e, f = [None] * last, [None] * last
    e[last - 1] = t[last - 1] * i[last - 1]
    f[last - 1] = u[last - 1]
    for m in reversed(range(last - 1)):
        e[m] = t[m] * i[m] - u[m] * e[m + 1]
        f[m] = -u[m] * f[m + 1]
    for m in range(last):
        out["i%d" % m], out["e%d" % m], out["f%d" % m] = i[m], e[m], f[m]
        if m:
            out["w%d" % m] = w[m]
        if m < last - 1:
            out["u%d" % m] = u[m]
    out["a7"], out["c7"] = a[last], c[last]
    out["en"], out["fn"] = lane_roll(e[0], -1), lane_roll(f[0], -1)
    low = -a[last] * e[last - 1]
    mid = b[last] - a[last] * f[last - 1] - c[last] * out["en"]
    high = -c[last] * out["fn"]
    for level in range(3):
        k = 1 << (2 * level)
        pairs = []
        for reach in (k, 2 * k):
            inv = 1.0 / mid
            al = -low * lane_roll(inv, reach)
            ga = -high * lane_roll(inv, -reach)
            mid = mid + al * lane_roll(high, reach) + ga * lane_roll(low, -reach)
            low, high = al * lane_roll(low, reach), ga * lane_roll(high, -reach)
            pairs.append((al, ga))
        (al1, ga1), (al2, ga2) = pairs
        merged = {
            "d1": al1 + al2 * lane_roll(ga1, 2 * k), "d2": al2, "d3": al2 * lane_roll(al1, 2 * k),
            "u1": ga1 + ga2 * lane_roll(al1, -2 * k), "u2": ga2, "u3": ga2 * lane_roll(ga1, -2 * k),
        }
        for key, value in merged.items():
            out["p%d%s" % (level, key)] = value
    inv = 1.0 / mid
    out["inv"] = inv
    for key in ("d1", "d2", "d3", "u1", "u2", "u3"):
        out["p2" + key] = out["p2" + key] * inv
    return out


def least_squares(columns, initial):
    count = len(columns)
    cosines, sines = [], []
    rhs = [initial] + [None] * count
    upper = []
    for position in range(count):
        column = list(columns[position])
        for earlier in range(position):
            first = cosines[earlier] * column[earlier] + sines[earlier] * column[earlier + 1]
            second = -sines[earlier] * column[earlier] + cosines[earlier] * column[earlier + 1]
            column[earlier], column[earlier + 1] = first, second
        radius = jnp.sqrt(column[position] * column[position] + column[position + 1] * column[position + 1])
        inverse = 1.0 / radius
        cosine = column[position] * inverse
        sine = column[position + 1] * inverse
        cosines.append(cosine)
        sines.append(sine)
        rhs[position + 1] = -sine * rhs[position]
        rhs[position] = cosine * rhs[position]
        upper.append(column[:position] + [inverse])
    y = [None] * count
    for position in reversed(range(count)):
        accum = rhs[position]
        for onward in range(position + 1, count):
            accum = accum - upper[onward][position] * y[onward]
        y[position] = accum * upper[position][position]
    return y


def solve_weights(gram):
    n = ITERS + 1
    r = {}
    for i in range(n):
        pivot = gram[(i, i)]
        for m in range(i):
            pivot = pivot - r[(m, i)] * r[(m, i)]
        pivot = jnp.maximum(pivot, gram[(i, i)] * 1e-9)
        root = jnp.sqrt(pivot)
        r[(i, i)] = root
        inverse = 1.0 / root
        for j in range(i + 1, n):
            value = gram[(i, j)]
            for m in range(i):
                value = value - r[(m, i)] * r[(m, j)]
            r[(i, j)] = value * inverse
    columns = []
    for k in range(ITERS):
        columns.append([r[(i, k)] + r[(i, k + 1)] for i in range(k + 1)] + [r[(k + 1, k + 1)]])
    return least_squares(columns, r[(0, 0)])


def kernel(chips, shifts_hbm, stiff_hbm, mass_hbm, factor_hbm, low_hbm, res_hbm,
           perm, own_s, own_m, own_w, lhs, send_c, send_w, raw_c, ce, fc, pb, zb, ub, mz, zn, os_, arb, hx, msg, shifts,
           own_sem, in_send, in_recv, far_send, ar_send, ar_recv, hx_send, hx_recv, out_send, out_recv, out_local):
    me = lax.axis_index("rows")
    k = me // 2
    c = me % 2
    up = lax.rem(k + chips - 1, chips)
    down = lax.rem(k + 1, chips)

    def device(chip, core):
        return (chip * 2 + core,)

    barrier = pltpu.get_barrier_semaphore()

    if chips == 64:
        ahead = [[lax.rem(lax.div(k, stride) + n, 4) * stride for n in range(4)] for stride in (16, 4, 1)]
        spans = sorted(
            ((a, b, d) for a in range(4) for b in range(4) for d in range(4) if (a, b, d) != (0, 0, 0)),
            key=lambda offset: -sum(min(n, 4 - n) for n in offset))
        others = [ahead[0][a] + ahead[1][b] + ahead[2][d] for a, b, d in spans]
    else:
        others = [lax.rem(k + n, chips) for n in range(1, chips)]

    for chip in (up, down, k):
        pl.semaphore_signal(barrier, inc=1, device_id=device(chip, 1 - c), device_id_type=MESH)
    for chip in others:
        pl.semaphore_signal(barrier, inc=1, device_id=device(chip, c), device_id_type=MESH)

    own_copies = [
        pltpu.make_async_copy(stiff_hbm, own_s, own_sem.at[0]),
        pltpu.make_async_copy(mass_hbm, own_m, own_sem.at[1]),
        pltpu.make_async_copy(factor_hbm, own_w, own_sem.at[2]),
        pltpu.make_async_copy(shifts_hbm, shifts, own_sem.at[3]),
    ]
    for copy in own_copies:
        copy.start()

    row = lax.broadcasted_iota(jnp.int32, (512, 512), 0)
    col = lax.broadcasted_iota(jnp.int32, (512, 512), 1)
    perm[...] = jnp.where(row == CHUNK * (col % HALF) + col // HALF, 1.0, 0.0).astype(BF16)

    lane = lax.broadcasted_iota(jnp.int32, (8, LANES), 1)
    left = lane < HALF
    sub = lax.broadcasted_iota(jnp.int32, (8, LANES), 0)
    halves8 = jnp.where((sub % 2 == 0) == left, 1.0, 0.0).astype(BF16)
    sub16 = lax.broadcasted_iota(jnp.int32, (16, LANES), 0)
    lane16 = lax.broadcasted_iota(jnp.int32, (16, LANES), 1)
    halves16 = jnp.where(sub16 == lane16 // HALF, 1.0, 0.0).astype(BF16)
    lane1 = lax.broadcasted_iota(jnp.int32, (1, LANES), 1)
    left1 = lane1 < HALF
    first = k == 0
    last = k == chips - 1
    own = 2 + c

    for copy in own_copies:
        copy.wait()
    for e in range(18):
        lhs[4 * e:4 * e + 4, :] = own_s[e] if e < 9 else own_m[e - 9]
    send_c[...] = permuted(lhs[0:72, :], perm[...])
    moved = permuted(own_w[...].reshape(128, 512), perm[...])
    for core in range(2):
        for r in range(4):
            at = 32 * r + 16 * core
            for q in range(4):
                one = moved[at:at + 8, q * LANES:(q + 1) * LANES]
                two = moved[at + 8:at + 16, q * LANES:(q + 1) * LANES]
                send_w[core, r, 2 * q] = jnp.where(left, one, lane_roll(two, HALF))
                send_w[core, r, 2 * q + 1] = jnp.where(left, lane_roll(one, HALF), two)
    raw_c[own] = send_c[...]
    pb[0, pl.ds(4 * own, 4)] = send_w[c]

    pl.semaphore_wait(barrier, chips - 1 + 3)

    def block_copies(chip, core, block, sems):
        return [
            pltpu.make_async_remote_copy(
                src_ref=send_c, dst_ref=raw_c.at[block],
                send_sem=sems.at[0], recv_sem=in_recv.at[block, 0], device_id=device(chip, core), device_id_type=MESH),
            pltpu.make_async_remote_copy(
                src_ref=send_w.at[core], dst_ref=pb.at[0, pl.ds(4 * block, 4)],
                send_sem=sems.at[1], recv_sem=in_recv.at[block, 1], device_id=device(chip, core), device_id_type=MESH),
        ]

    near_chip = lax.rem(k + 2 * c - 1 + chips, chips)
    far_chip = lax.rem(k + 1 - 2 * c + chips, chips)
    near_copies, far_copies = [], []
    for core in range(2):
        near_copies.append(block_copies(near_chip, core, 4 - 3 * c, in_send.at[core]))
        far_copies += block_copies(far_chip, core, 5 * c, far_send.at[core])
    near_copies.append(block_copies(k, 1 - c, own, in_send.at[2]))
    near_copies = [pair[0] for pair in near_copies] + [pair[1] for pair in near_copies]
    for copy in near_copies:
        copy.start()

    def wait_stencil(block):
        pltpu.make_async_copy(raw_c.at[block], raw_c.at[block], in_recv.at[block, 0]).wait()

    def wait_field(block):
        rows = pb.at[0, pl.ds(4 * block, 4)]
        pltpu.make_async_copy(rows, rows, in_recv.at[block, 1]).wait()

    def absent(block):
        if block < 2:
            return first
        if block > 3:
            return last
        return None

    def prepare(blocks, base):
        count = 4 * len(blocks)
        for e in range(18):
            for n, block in enumerate(blocks):
                value = raw_c[block, 4 * e:4 * e + 4, :]
                gone = absent(block)
                if gone is not None:
                    value = jnp.where(gone, 1.0 if e == 4 else 0.0, value)
                lhs[e * count + 4 * n:e * count + 4 * n + 4, :] = value
        for e in range(18):
            for q in range(4):
                value = lhs[e * count:(e + 1) * count, q * LANES:(q + 1) * LANES]
                other = lane_roll(value, HALF)
                both = [jnp.where(left1, value, other), jnp.where(left1, other, value)]
                if q == 0 and e % 3 == 0:
                    both[0] = jnp.where(lane1 % HALF == 0, 0.0, both[0])
                if q == 3 and e % 3 == 2:
                    both[1] = jnp.where(lane1 % HALF == HALF - 1, 0.0, both[1])
                for n in range(2):
                    ce[e * CHUNK + 2 * q + n, base:base + count, :] = both[n]

    def clear(block):
        @pl.when(absent(block))
        def _():
            pb[0, 4 * block:4 * block + 4] = jnp.zeros((4, CHUNK, 8, LANES), F32)

    def factor_rows(t, lo, hi):
        s = shifts[t]
        par = lax.rem(t, 2)

        def entry(e, m):
            return ce[e * CHUNK + m, lo:hi, :] + s * ce[(9 + e) * CHUNK + m, lo:hi, :]
        parts = line_factors(*[[entry(e, m) for m in range(CHUNK)] for e in (3, 4, 5)])
        for name, value in parts.items():
            fc[par, SLOT[name], lo:hi, :] = value
        for n, e in enumerate(OFF):
            for m in range(CHUNK):
                fc[par, len(NAMES) + n * CHUNK + m, lo:hi, :] = entry(e, m)

    def slot_of(r):
        if isinstance(r, int):
            return r + 16 if r < 4 else (r - 4 if r < 20 else r)
        return jnp.where(r < 4, r + 16, jnp.where(r < 20, r - 4, r))

    def line_group(par, it, rows):
        slots = [slot_of(r) for r in rows]

        def co(name, n):
            return fc[par, SLOT[name], pl.ds(slots[n], 1), :]

        g, d, ahead_g = [], [], []
        for n, r in enumerate(rows):
            v = [pb[it, r, m] for m in range(CHUNK)]
            for m in range(1, CHUNK - 1):
                v[m] = v[m] - co("w%d" % m, n) * v[m - 1]
            x = [v[m] * co("i%d" % m, n) for m in range(CHUNK - 1)]
            for m in reversed(range(CHUNK - 2)):
                x[m] = x[m] - co("u%d" % m, n) * x[m + 1]
            ahead_g.append(lane_roll(x[0], -1))
            d.append(v[-1] - co("a7", n) * x[-1] - co("c7", n) * ahead_g[-1])
            g.append(x)
        for level in range(3):
            step = 1 << (2 * level)
            new = []
            for n, v in enumerate(d):
                total = v if level < 2 else v * co("inv", n)
                for reach in (1, 2, 3):
                    total = total + (co("p%dd%d" % (level, reach), n) * lane_roll(v, reach * step)
                                     + co("p%du%d" % (level, reach), n) * lane_roll(v, -reach * step))
                new.append(total)
            d = new
        for n, r in enumerate(rows):
            after = d[n]
            before = lane_roll(after, 1)
            zb[it, r, 0] = before
            zb[it, r, CHUNK] = after
            for m in range(CHUNK - 1):
                zb[it, r, m + 1] = g[n][m] - co("e%d" % m, n) * before - co("f%d" % m, n) * after
            zb[it, r, CHUNK + 1] = ahead_g[n] - co("en", n) * after - co("fn", n) * lane_roll(after, -1)

    def off_row(par, it, r):
        slot = slot_of(r)
        for m in range(CHUNK):
            total = None
            for n, e in enumerate(OFF):
                source = zb[it, r + (-1 if e < 3 else 1), m + e % 3]
                term = fc[par, len(NAMES) + n * CHUNK + m, pl.ds(slot, 1), :] * source
                total = term if total is None else total + term
            pb[it + 1, r, m] = total

    def mass_row(it, n):
        for m in range(CHUNK):
            total = None
            for e in range(9):
                term = ce[(9 + e) * CHUNK + m, pl.ds(n + 4, 1), :] * zb[it, n + 7 + e // 3, m + e % 3]
                total = term if total is None else total + term
            mz[it, n, m] = total

    def send_halo(do):
        for n, (chip, at) in enumerate(((down, 8), (up, 12))):
            copy = pltpu.make_async_remote_copy(
                src_ref=pb.at[0, pl.ds(at, 4)], dst_ref=hx.at[n], send_sem=hx_send.at[n], recv_sem=hx_recv.at[n],
                device_id=device(chip, c), device_id_type=MESH)
            do(copy)

    def ar_copy(t, chip):
        return pltpu.make_async_remote_copy(
            src_ref=msg.at[t], dst_ref=arb.at[t, k], send_sem=ar_send.at[t], recv_sem=ar_recv.at[t],
            device_id=device(chip, c), device_id_type=MESH)

    def out_copies(n, dst):
        return (
            pltpu.make_async_copy(os_.at[n, pl.ds(4 * c, 4)], dst, out_local.at[n]),
            pltpu.make_async_remote_copy(
                src_ref=os_.at[n, pl.ds(4 - 4 * c, 4)], dst_ref=dst, send_sem=out_send.at[n], recv_sem=out_recv.at[n],
                device_id=device(k, 1 - c), device_id_type=MESH),
        )

    half_cols = pl.ds(pl.multiple_of(16 * c, 16), 16)

    def out_ref(n):
        return low_hbm.at[n, :, half_cols, :]

    def native(source):
        whole = left[None]
        tiles = [[], []]
        for q in range(4):
            even, odd = source[:, 2 * q], source[:, 2 * q + 1]
            tiles[0].append(jnp.where(whole, even, lane_roll(odd, HALF)).reshape(64, LANES))
            tiles[1].append(jnp.where(whole, lane_roll(even, HALF), odd).reshape(64, LANES))
        flat = jnp.concatenate([jnp.concatenate(t, axis=1) for t in tiles], axis=0)
        return permuted(flat, perm[...], 1).reshape(2, 8, 8, 512)

    def emit(n, source, dst):
        halves = native(source)
        for h in range(2):
            os_[n, :, 8 * h:8 * h + 8, :] = halves[h]
        for copy in out_copies(n, dst):
            copy.start()

    def emit_low(n):
        scale = jnp.sqrt(jnp.full((1, 1, 8, LANES), 2.0 * shifts[n], F32))
        emit(n, scale * ub[8:16, 1:CHUNK + 1], out_ref(n))

    for block in (2, 3):
        @pl.when(block == 3 - c)
        def _():
            wait_stencil(block)
    wait_stencil(1)
    wait_stencil(4)
    for copy in far_copies:
        copy.start()
    prepare((1, 2, 3, 4), 0)
    factor_rows(0, 0, 16)
    for block in (2, 3):
        @pl.when(block == 3 - c)
        def _():
            wait_field(block)
    for block in (1, 4):
        wait_field(block)
        clear(block)

    def adi(t, carry):
        s = shifts[t]
        par = lax.rem(t, 2)

        sums = {pair: jnp.zeros((8, LANES), F32) for pair in PAIRS}

        def dots(latest):
            for r in range(8, 16):
                for m in range(CHUNK):
                    newest = pb[latest, r, m]
                    for i in range(latest + 1):
                        sums[(i, latest)] = sums[(i, latest)] + newest * (newest if i == latest else pb[i, r, m])

        for it in range(ITERS):
            line_group(par, it, list(range(4 + it, 20 - it)))
            dots(it)

            for r in range(5 + it, 19 - it):
                off_row(par, it, r)
        dots(ITERS)
        stacked = jnp.concatenate([sums[pair] for pair in PAIRS] + [jnp.zeros((8, LANES), F32)], axis=0)
        packed = lax.dot_general(halves16, jnp.concatenate(split3(stacked), axis=0), (((1,), (1,)), ((), ())), preferred_element_type=F32)
        packed = packed[0:2, 0:LANES] + packed[0:2, LANES:2 * LANES] + packed[0:2, 2 * LANES:]
        msg[t] = packed
        arb[t, k] = packed

        for chip in others:
            ar_copy(t, chip).start()

        @pl.when(t < 2)
        def _():
            factor_rows(t + 1, 0, 16)

        @pl.when(t > 0)
        def _():
            emit_low(t - 1)

        @pl.when(t == 0)
        def _():
            for block in (0, 5):
                wait_stencil(block)
            prepare((0, 5), 16)
            factor_rows(0, 16, 24)
            factor_rows(1, 16, 24)
            for block in (0, 5):
                wait_field(block)
                clear(block)

        @pl.when(t == 1)
        def _():
            send_halo(lambda copy: copy.wait())
            for n, at in enumerate((0, 20)):
                gone = first if n == 0 else last
                for r in range(4):
                    pb[0, at + r] = jnp.where(gone, 0.0, hx[n, r])

        @pl.when(t < 2)
        def _():
            def outer(it, carry):
                line_group(par, it, [it + n for n in range(4)] + [20 - it + n for n in range(4)])

                @pl.when(it < ITERS - 1)
                def _():
                    def rows(n, carry):
                        off_row(par, it, it + 1 + n)
                        off_row(par, it, 19 - it + n)
                        return carry
                    lax.fori_loop(0, 4, rows, 0)
                return carry
            lax.fori_loop(0, ITERS, outer, 0)

        @pl.when(t == STEPS - 1)
        def _():
            def images(n, carry):
                mass_row(n // 4, 2 * (n % 4))
                mass_row(n // 4, 2 * (n % 4) + 1)
                return carry
            lax.fori_loop(0, 4 * ITERS, images, 0)

            def reorder(it, carry):
                zn[it] = native(zb[it, 8:16, 1:CHUNK + 1])
                zn[ITERS + it] = native(mz[it])
                return carry
            lax.fori_loop(0, ITERS, reorder, 0)
            zn[2 * ITERS] = native(pb[0, 8:16])

        pltpu.make_async_copy(arb.at[t, pl.ds(0, chips - 1)], arb.at[t, pl.ds(0, chips - 1)], ar_recv.at[t]).wait()
        total = jnp.sum(arb[t], axis=0)
        total = jnp.concatenate([total] * 3 + [jnp.zeros((2, LANES), F32)], axis=0)
        one, two, three = [part.astype(F32) for part in split3(total)]
        total = jnp.where(sub < 2, one, jnp.where(sub < 4, two, three)).astype(BF16)
        spread_out = lax.dot_general(total, halves8, (((0,), (0,)), ((), ())), preferred_element_type=F32)
        gram = {pair: spread_out[8 * n:8 * n + 8] for n, pair in enumerate(PAIRS)}
        y = solve_weights(gram)

        def combine(r, carry):
            for m in range(CHUNK + 2):
                total = y[0] * zb[0, r, m]
                for it in range(1, ITERS):
                    total = total + y[it] * zb[it, r, m]
                ub[r, m] = total
            return carry

        twice = 2.0 * s

        def update(r, carry):
            slot = slot_of(r)
            for m in range(CHUNK):
                total = None
                for e in range(9):
                    term = ce[(9 + e) * CHUNK + m, pl.ds(slot, 1), :] * ub[r + e // 3 - 1, m + e % 3]
                    total = term if total is None else total + term
                pb[0, r, m] = pb[0, r, m] - twice * total
            return carry
        @pl.when(t < STEPS - 1)
        def _():
            for r in range(7, 17):
                combine(r, 0)
            for r in range(8, 16):
                update(r, 0)

        @pl.when(t == 0)
        def _():
            send_halo(lambda copy: copy.start())

        @pl.when(t < STEPS - 1)
        def _():
            for r in list(range(3, 7)) + list(range(17, 21)):
                combine(r, 0)
            for r in list(range(4, 8)) + list(range(16, 20)):
                update(r, 0)

        @pl.when(t == STEPS - 1)
        def _():
            both = []
            for value in y:
                other = lane_roll(value, HALF)
                both.append((jnp.where(left, value, other), jnp.where(left, other, value)))
            scale = jnp.sqrt(jnp.full((8, LANES), twice, F32))

            def weighted(base, factor, h, r, span):
                total = (factor * both[0][h]) * zn[base, h, r, :, span]
                for it in range(1, ITERS):
                    total = total + (factor * both[it][h]) * zn[base + it, h, r, :, span]
                return total

            def low_row(r, carry):
                for h in range(2):
                    for q in range(4):
                        span = slice(q * LANES, (q + 1) * LANES)
                        os_[STEPS - 1, r, 8 * h:8 * h + 8, span] = weighted(0, scale, h, r, span)
                return carry

            def res_row(r, carry):
                for h in range(2):
                    for q in range(4):
                        span = slice(q * LANES, (q + 1) * LANES)
                        os_[STEPS, r, 8 * h:8 * h + 8, span] = zn[2 * ITERS, h, r, :, span] - weighted(ITERS, twice, h, r, span)
                return carry
            lax.fori_loop(0, 8, low_row, 0, unroll=2)
            for copy in out_copies(STEPS - 1, out_ref(STEPS - 1)):
                copy.start()
            lax.fori_loop(0, 8, res_row, 0, unroll=2)
            for copy in out_copies(STEPS, res_at):
                copy.start()
        return carry

    res_at = res_hbm.at[:, half_cols, :]
    lax.fori_loop(0, STEPS, adi, 0)

    for copy in near_copies + far_copies:
        copy.wait_send()

    def drain(t, carry):
        pltpu.make_async_copy(arb.at[t, pl.ds(0, chips - 1)], arb.at[t, pl.ds(0, chips - 1)], ar_send.at[t]).wait()
        for copy in out_copies(t, out_ref(t)):
            copy.wait()
        return carry
    lax.fori_loop(0, STEPS, drain, 0)
    for copy in out_copies(STEPS, res_at):
        copy.wait()


def solution(mesh):
    chips = mesh.shape["rows"] // 2

    def shards(stiffness, mass, shifts, factor):
        field = (24, CHUNK, 8, LANES)
        framed = (24, CHUNK + 2, 8, LANES)
        dma = pltpu.SemaphoreType.DMA
        return pl.pallas_call(
            functools.partial(kernel, chips),
            out_shape=(jax.ShapeDtypeStruct((STEPS, 4, 32, 512), F32), jax.ShapeDtypeStruct((4, 32, 512), F32)),
            in_specs=[pl.BlockSpec(memory_space=pl.ANY)] * 4,
            out_specs=(pl.BlockSpec(memory_space=pl.ANY), pl.BlockSpec(memory_space=pl.ANY)),
            scratch_shapes=[
                pltpu.VMEM((512, 512), BF16),
                pltpu.VMEM((9, 4, 512), F32),
                pltpu.VMEM((9, 4, 512), F32),
                pltpu.VMEM((4, 32, 512), F32),
                pltpu.VMEM((18 * 16, 512), F32),
                pltpu.VMEM((18 * 4, 512), F32),
                pltpu.VMEM((2, 4, CHUNK, 8, LANES), F32),
                pltpu.VMEM((6, 18 * 4, 512), F32),
                pltpu.VMEM((18 * CHUNK, 24, LANES), F32),
                pltpu.VMEM((2, COUNT, 24, LANES), F32),
                pltpu.VMEM((ITERS + 1,) + field, F32),
                pltpu.VMEM((ITERS,) + framed, F32),
                pltpu.VMEM(framed, F32),
                pltpu.VMEM((ITERS, 8, CHUNK, 8, LANES), F32),
                pltpu.VMEM((2 * ITERS + 1, 2, 8, 8, 512), F32),
                pltpu.VMEM((STEPS + 1, 8, 16, 512), F32),
                pltpu.VMEM((STEPS, chips, 2, LANES), F32),
                pltpu.VMEM((2, 4, CHUNK, 8, LANES), F32),
                pltpu.VMEM((STEPS, 2, LANES), F32),
                pltpu.SMEM((STEPS,), F32),
                dma((4,)),
                dma((3, 2)),
                dma((6, 2)),
                dma((2, 2)),
                dma((STEPS,)),
                dma((STEPS,)),
                dma((2,)),
                dma((2,)),
                dma((STEPS + 1,)),
                dma((STEPS + 1,)),
                dma((STEPS + 1,)),
            ],
            compiler_params=pltpu.CompilerParams(
                collective_id=0, has_side_effects=True, vmem_limit_bytes=60 << 20),
        )(shifts, stiffness, mass, factor)

    return jax.shard_map(
        shards,
        mesh=mesh,
        in_specs=(P(None, "rows", None), P(None, "rows", None), P(), P("rows", None, None)),
        out_specs=(P(None, "rows", None, None), P("rows", None, None)),
        check_vma=False,
    )
```
